256 devices in a mesh: seq: 8 (over y, core), fsdp: 16 (over z_hi, x), tp: 2 (over z_lo).
Axes of the slice: x: 4, y: 4, z: 8 (z_hi: 4, z_lo: 2; z = z_hi * 2 + z_lo), core: 2. Of those that a mesh axis runs over, the one named last changes fastest.
Arguments:
- hidden: bfloat16 [16, 1024, 8192], P('fsdp', 'seq'), may hold values from -6 to 6
- queries: bfloat16 [16, 1024, 8192], P('fsdp', 'seq', 'tp'), may hold values from -600 to 600
- w_kv: bfloat16 [2, 8192, 1024], P(None, 'fsdp', 'tp'), may hold values from -0.0625 to 0.0625
- b_kv: bfloat16 [2, 1024], P(None, 'tp'), may hold values from -3 to 3
- doc_starts: int32 [16, 2], P('fsdp'), may hold values from 0 to 896, as said below
- block_docs: int32 [16, 8], P('fsdp'), may hold values from 0 to 1, as said below
Outputs:
- attended: bfloat16 [16, 1024, 8192], P('fsdp', 'seq', 'tp')
The draws below stay inside these ranges and needn't reach their ends.
Inputs may be any that keep to these rules, and one draw needn't show every extreme that they name: `doc_starts`: each row holds exactly 2 documents of whole blocks of 128 tokens, starts rising from 0; one document of each row has exactly 6 blocks. `block_docs`: the document of each block, matching doc_starts.
All inputs are finite; a program needn't handle non-finite values.
Results may differ from the reference program's by a relative error of at most 0.015.
Values may be sent and summed in bfloat16 or wider, within the bound.
A program may use at most 128 MiB of HBM per device.

```python
import jax
import jax.numpy as jnp
from jax import lax

D = 8192
HQ = 64
KV = 8
HD = 128
BLK = 128
LEN = 1024
ROWS = 16
NDOC = 2


def doc_layout(key):
    nblocks = LEN // BLK
    longest = 3 * nblocks // 4
    extra = nblocks - longest - (NDOC - 1)
    base = jax.random.fold_in(key, 4242)
    key_long, key_picks = jax.random.split(base)
    long_index = jax.random.randint(key_long, (ROWS,), 0, NDOC)
    picks = jax.random.randint(key_picks, (ROWS, extra + 1), 0, NDOC - 1)[:, :extra]
    counts = jnp.sum((picks[:, :, None] == jnp.arange(NDOC - 1)[None, None, :]).astype(jnp.int32), axis=1)
    others = 1 + counts
    index = jnp.arange(NDOC, dtype=jnp.int32)[None, :]
    source = index - (index > long_index[:, None]).astype(jnp.int32)
    source = jnp.clip(source, 0, NDOC - 2)
    spread = jnp.take_along_axis(others, source, axis=1)
    lengths = jnp.where(index == long_index[:, None], longest, spread).astype(jnp.int32)
    start_blocks = jnp.cumsum(lengths, axis=1) - lengths
    return start_blocks.astype(jnp.int32)


def draw_doc_starts(key, part):
    return (doc_layout(key) * BLK).astype(jnp.int32)


def draw_block_docs(key, part):
    start_blocks = doc_layout(key)
    nblocks = LEN // BLK
    blocks = jnp.arange(nblocks, dtype=jnp.int32)
    inside = (start_blocks[:, None, :] <= blocks[None, :, None]).astype(jnp.int32)
    return (jnp.sum(inside, axis=2) - 1).astype(jnp.int32)


def draw_queries(key, part):
    key_base = jax.random.fold_in(key, 0)
    shape = (ROWS, LEN, HQ * HD)
    values = jnp.clip(2.0 * jax.random.normal(key_base, shape, jnp.float32), -12.0, 12.0)
    return values.astype(jnp.bfloat16)


def level_of(stream_key, dims, pieces, smallest, largest):
    factor_of, own = 1.0, jax.random.fold_in(stream_key, 6)
    for dim, parts in pieces:
        heights = jnp.exp(jax.random.uniform(jax.random.fold_in(own, dim), (parts,), jnp.float32, smallest / len(pieces), largest / len(pieces)))
        factor_of = factor_of * jnp.repeat(heights, dims[dim] // parts).reshape([-1 if axis == dim else 1 for axis in range(len(dims))])
    return factor_of


def scatter_about(rng, dims, scale, bound, cuts=(), held_as=jnp.bfloat16):
    gain = level_of(rng, dims, cuts, -0.22, 0.18) if cuts else 1.0
    values = jax.random.normal(rng, dims, jnp.float32) * scale * gain
    return jnp.minimum(jnp.maximum(values, -bound), bound).astype(held_as)


def setup_inputs(seed: int = 0) -> dict:
    arg_keys = jax.random.split(jax.random.key(seed), 7)
    return {
        "hidden": scatter_about(arg_keys[0], (ROWS, LEN, D), 1.0, 6.0, ((0, 16), (1, 8))),
        "queries": draw_queries(jax.random.fold_in(arg_keys[6], 71), 0),
        "w_kv": scatter_about(arg_keys[2], (2, D, KV * HD), D ** -0.5, 0.0625, ((1, 16), (2, 2))),
        "b_kv": scatter_about(arg_keys[3], (2, KV * HD), 0.5, 3.0, ((1, 2),)),
        "doc_starts": draw_doc_starts(jax.random.fold_in(arg_keys[6], 71), 0),
        "block_docs": draw_block_docs(jax.random.fold_in(arg_keys[6], 71), 0),
    }


def rotate_keys(key_heads, positions):
    half = HD // 2
    freqs = jnp.exp(-jnp.arange(half, dtype=jnp.float32) * (2.0 / HD) * jnp.log(jnp.float32(1000000.0)))
    angle = positions.astype(jnp.float32)[:, None] * freqs[None, :]
    cosine = jnp.cos(angle)[:, None, :]
    sine = jnp.sin(angle)[:, None, :]
    first = key_heads[..., :half]
    second = key_heads[..., half:]
    return jnp.concatenate([first * cosine - second * sine, second * cosine + first * sine], axis=-1)

def reference(hidden, queries, w_kv, b_kv, doc_starts, block_docs):
    group = HQ // KV
    inv_root = 1.0 / jnp.sqrt(jnp.float32(HD))

    def one_row(packed):
        row_hidden, row_queries, starts, blocks = packed
        projected = jnp.einsum('td,cde->cte', row_hidden.astype(jnp.float32), w_kv.astype(jnp.float32))
        projected = projected + b_kv.astype(jnp.float32)[:, None, :]
        tokens = jnp.arange(LEN, dtype=jnp.int32)
        docs = blocks[tokens // BLK]
        positions = tokens - starts[docs]
        keys = rotate_keys(projected[0].reshape(LEN, KV, HD), positions).astype(jnp.bfloat16)
        values = projected[1].reshape(LEN, KV, HD).astype(jnp.bfloat16)
        query_heads = row_queries.reshape(LEN, KV, group, HD)
        same_doc = docs[:, None] == docs[None, :]

        def one_head(head):
            query_part = query_heads[:, head].astype(jnp.float32)
            key_part = keys[:, head].astype(jnp.float32)
            value_part = values[:, head].astype(jnp.float32)
            scores = jnp.einsum('tjd,sd->jts', query_part, key_part) * inv_root
            scores = jnp.where(same_doc[None], scores, jnp.float32(-1e+30))
            top = lax.optimization_barrier(jnp.max(scores, axis=-1, keepdims=True))
            weight = jnp.where(same_doc[None], jnp.exp(scores - top), jnp.float32(0.0))
            total = lax.optimization_barrier(jnp.sum(weight, axis=-1))
            weight_b = lax.optimization_barrier(weight.astype(jnp.bfloat16))
            summed = jnp.einsum('jts,sd->tjd', weight_b.astype(jnp.float32), value_part)
            return summed / jnp.transpose(total)[:, :, None]
        heads_out = lax.map(one_head, jnp.arange(KV, dtype=jnp.int32))
        return jnp.transpose(heads_out, (1, 0, 2, 3)).reshape(LEN, HQ * HD).astype(jnp.bfloat16)
    return lax.map(one_row, (hidden, queries, doc_starts, block_docs))
```

```python
import jax
import jax.numpy as jnp
from jax import lax
from jax.sharding import Mesh
from jax.sharding import PartitionSpec as P

HD = 128
BLK = 128

SEQ = ("sy", "sc")
FSDP = ("fz", "fx")


def rotate_keys(key_heads, positions):
    half = key_heads.shape[-1] // 2
    freqs = jnp.exp(
        -jnp.arange(half, dtype=jnp.float32)
        * (2.0 / key_heads.shape[-1])
        * jnp.log(jnp.float32(1000000.0))
    )
    angle = positions.astype(jnp.float32)[:, None] * freqs[None, :]
    cosine = jnp.cos(angle)[:, None, :]
    sine = jnp.sin(angle)[:, None, :]
    first = key_heads[..., :half]
    second = key_heads[..., half:]
    return jnp.concatenate(
        [first * cosine - second * sine, second * cosine + first * sine], axis=-1
    )


def lookup_docs(token_index, block_table):
    block_index = token_index // BLK
    matches = block_index[:, None] == jnp.arange(block_table.shape[0], dtype=jnp.int32)[None, :]
    return jnp.sum(jnp.where(matches, block_table[None, :], 0), axis=1)


def doc_positions(token_index, doc_starts, block_docs):
    docs = lookup_docs(token_index, block_docs[0])
    doc_match = docs[:, None] == jnp.arange(doc_starts.shape[1], dtype=jnp.int32)[None, :]
    doc_first = jnp.sum(jnp.where(doc_match, doc_starts[0][None, :], 0), axis=1)
    return docs, token_index - doc_first


def make_per_device(cores):
    def per_device(hidden, queries, w_kv, b_kv, doc_starts, block_docs):
        tok_count = hidden.shape[1]
        core = lax.axis_index("sc")
        chip = lax.axis_index("sy")
        cols = w_kv.shape[2] // cores
        w_part = lax.dynamic_slice_in_dim(w_kv, core * cols, cols, axis=2)
        b_part = lax.dynamic_slice_in_dim(b_kv, core * cols, cols, axis=1)
        chip_rows = lax.all_gather(hidden[0], "sc", axis=0, tiled=True)
        chip_tokens = chip_rows.shape[0]
        key_value = jnp.einsum(
            "td,cde->cte",
            chip_rows,
            lax.all_gather(w_part, FSDP, axis=1, tiled=True),
            preferred_element_type=jnp.float32,
        )
        key_value = key_value + b_part.astype(jnp.float32)[:, None, :]
        chip_pos = chip * chip_tokens + jnp.arange(chip_tokens, dtype=jnp.int32)
        _, positions = doc_positions(chip_pos, doc_starts, block_docs)
        part_heads = cols // HD
        rotated = rotate_keys(key_value[0].reshape(chip_tokens, part_heads, HD), positions)
        keys = rotated.astype(jnp.bfloat16).reshape(chip_tokens, cols)
        values = key_value[1].astype(jnp.bfloat16)
        stacked = jnp.stack([keys, values])
        gathered = lax.all_gather(stacked, SEQ, axis=0, tiled=False)
        chips = gathered.shape[0] // cores
        gathered = gathered.reshape(chips, cores, 2, chip_tokens, cols)
        piece = jnp.transpose(gathered, (2, 0, 3, 1, 4)).reshape(2, chips * chip_tokens, cores * cols)

        seq_pos = (chip * cores + core) * tok_count + jnp.arange(tok_count, dtype=jnp.int32)
        query_docs = lookup_docs(seq_pos, block_docs[0])
        key_heads = piece.shape[2] // HD
        group = queries.shape[2] // HD // key_heads
        query_heads = queries[0].reshape(tok_count, key_heads, group, HD)
        inv_root = 1.0 / jnp.sqrt(jnp.float32(HD))
        width = piece.shape[1]
        key_docs = lookup_docs(jnp.arange(width, dtype=jnp.int32), block_docs[0])
        same_doc = query_docs[:, None] == key_docs[None, :]
        run_max = jnp.full((key_heads, group, tok_count), -1e30, jnp.float32)
        key_part = piece[0].reshape(width, key_heads, HD)
        value_part = piece[1].reshape(width, key_heads, HD)
        scores = (
            jnp.einsum("tgjd,sgd->gjts", query_heads, key_part, preferred_element_type=jnp.float32)
            * inv_root
        )
        scores = jnp.where(same_doc[None, None], scores, jnp.float32(-1e30))
        new_max = jnp.maximum(run_max, jnp.max(scores, axis=-1))
        weight = jnp.where(same_doc[None, None], jnp.exp(scores - new_max[..., None]), jnp.float32(0.0))
        new_sum = jnp.sum(weight, axis=-1)
        update = jnp.einsum(
            "gjts,sgd->gjtd",
            weight.astype(jnp.bfloat16),
            value_part,
            preferred_element_type=jnp.float32,
        )
        result = update / new_sum[..., None]
        result = jnp.transpose(result, (2, 0, 1, 3)).reshape(tok_count, key_heads * group * HD)
        return result.astype(jnp.bfloat16)[None]

    return per_device


def solution(mesh):
    seq, fsdp, tp = (mesh.shape[name] for name in ("seq", "fsdp", "tp"))
    cores = 2
    x_size = 4
    fine = Mesh(
        mesh.devices.reshape(seq // cores, cores, fsdp // x_size, x_size, tp),
        ("sy", "sc", "fz", "fx", "tp"),
    )
    in_specs = (
        P(FSDP, SEQ, None),
        P(FSDP, SEQ, "tp"),
        P(None, FSDP, "tp"),
        P(None, "tp"),
        P(FSDP, None),
        P(FSDP, None),
    )
    out_specs = P(FSDP, SEQ, "tp")
    return jax.shard_map(
        make_per_device(cores), mesh=fine, in_specs=in_specs, out_specs=out_specs, check_vma=False
    )
```

```python
import jax
import jax.numpy as jnp
from jax import lax
from jax.sharding import Mesh
from jax.sharding import PartitionSpec as P

HD = 128
BLK = 128

SEQ = ("sy", "sc")
FSDP = ("fz", "fx")


def rotate_keys(key_heads, positions):
    half = key_heads.shape[-1] // 2
    freqs = jnp.exp(
        -jnp.arange(half, dtype=jnp.float32)
        * (2.0 / key_heads.shape[-1])
        * jnp.log(jnp.float32(1000000.0))
    )
    angle = positions.astype(jnp.float32)[:, None] * freqs[None, :]
    cosine = jnp.cos(angle)[:, None, :]
    sine = jnp.sin(angle)[:, None, :]
    first = key_heads[..., :half]
    second = key_heads[..., half:]
    return jnp.concatenate(
        [first * cosine - second * sine, second * cosine + first * sine], axis=-1
    )


def lookup_docs(token_index, block_table):
    block_index = token_index // BLK
    matches = block_index[:, None] == jnp.arange(block_table.shape[0], dtype=jnp.int32)[None, :]
    return jnp.sum(jnp.where(matches, block_table[None, :], 0), axis=1)


def doc_positions(token_index, doc_starts, block_docs):
    docs = lookup_docs(token_index, block_docs[0])
    doc_match = docs[:, None] == jnp.arange(doc_starts.shape[1], dtype=jnp.int32)[None, :]
    doc_first = jnp.sum(jnp.where(doc_match, doc_starts[0][None, :], 0), axis=1)
    return docs, token_index - doc_first


def make_per_device(cores):
    def per_device(hidden, queries, w_kv, b_kv, doc_starts, block_docs):
        tok_count = hidden.shape[1]
        core = lax.axis_index("sc")
        chip = lax.axis_index("sy")
        cols = w_kv.shape[2] // cores
        w_part = lax.dynamic_slice_in_dim(w_kv, core * cols, cols, axis=2)
        b_part = lax.dynamic_slice_in_dim(b_kv, core * cols, cols, axis=1)
        own_rows = hidden[0]
        partner_rows = lax.ppermute(own_rows, "sc", [(i, (i + 1) % cores) for i in range(cores)])
        chip_rows = jnp.where(
            core == 0,
            jnp.concatenate([own_rows, partner_rows]),
            jnp.concatenate([partner_rows, own_rows]),
        )
        chip_tokens = chip_rows.shape[0]
        key_value = jnp.einsum(
            "td,cde->cte",
            chip_rows,
            lax.all_gather(w_part, FSDP, axis=1, tiled=True),
            preferred_element_type=jnp.float32,
        )
        key_value = key_value + b_part.astype(jnp.float32)[:, None, :]
        chip_pos = chip * chip_tokens + jnp.arange(chip_tokens, dtype=jnp.int32)
        _, positions = doc_positions(chip_pos, doc_starts, block_docs)
        part_heads = cols // HD
        rotated = rotate_keys(key_value[0].reshape(chip_tokens, part_heads, HD), positions)
        keys = rotated.astype(jnp.bfloat16).reshape(chip_tokens, cols)
        values = key_value[1].astype(jnp.bfloat16)
        stacked = jnp.stack([keys, values])
        gathered = lax.all_gather(stacked, SEQ, axis=0, tiled=False)
        chips = gathered.shape[0] // cores
        gathered = gathered.reshape(chips, cores, 2, chip_tokens, cols)
        piece = jnp.transpose(gathered, (2, 0, 3, 1, 4)).reshape(2, chips * chip_tokens, cores * cols)

        seq_pos = (chip * cores + core) * tok_count + jnp.arange(tok_count, dtype=jnp.int32)
        query_docs = lookup_docs(seq_pos, block_docs[0])
        key_heads = piece.shape[2] // HD
        group = queries.shape[2] // HD // key_heads
        query_heads = queries[0].reshape(tok_count, key_heads, group, HD)
        inv_root = 1.0 / jnp.sqrt(jnp.float32(HD))
        width = piece.shape[1]
        key_docs = lookup_docs(jnp.arange(width, dtype=jnp.int32), block_docs[0])
        same_doc = query_docs[:, None] == key_docs[None, :]
        run_max = jnp.full((key_heads, group, tok_count), -1e30, jnp.float32)
        key_part = piece[0].reshape(width, key_heads, HD)
        value_part = piece[1].reshape(width, key_heads, HD)
        scores = (
            jnp.einsum("tgjd,sgd->gjts", query_heads, key_part, preferred_element_type=jnp.float32)
            * inv_root
        )
        scores = jnp.where(same_doc[None, None], scores, jnp.float32(-1e30))
        new_max = jnp.maximum(run_max, jnp.max(scores, axis=-1))
        weight = jnp.where(same_doc[None, None], jnp.exp(scores - new_max[..., None]), jnp.float32(0.0))
        new_sum = jnp.sum(weight, axis=-1)
        update = jnp.einsum(
            "gjts,sgd->gjtd",
            weight.astype(jnp.bfloat16),
            value_part,
            preferred_element_type=jnp.float32,
        )
        result = update / new_sum[..., None]
        result = jnp.transpose(result, (2, 0, 1, 3)).reshape(tok_count, key_heads * group * HD)
        return result.astype(jnp.bfloat16)[None]

    return per_device


def solution(mesh):
    seq, fsdp, tp = (mesh.shape[name] for name in ("seq", "fsdp", "tp"))
    cores = 2
    x_size = 4
    fine = Mesh(
        mesh.devices.reshape(seq // cores, cores, fsdp // x_size, x_size, tp),
        ("sy", "sc", "fz", "fx", "tp"),
    )
    in_specs = (
        P(FSDP, SEQ, None),
        P(FSDP, SEQ, "tp"),
        P(None, FSDP, "tp"),
        P(None, "tp"),
        P(FSDP, None),
        P(FSDP, None),
    )
    out_specs = P(FSDP, SEQ, "tp")
    return jax.shard_map(
        make_per_device(cores), mesh=fine, in_specs=in_specs, out_specs=out_specs, check_vma=False
    )
```

```python
import jax
import jax.numpy as jnp
from jax import lax
from jax.sharding import Mesh
from jax.sharding import PartitionSpec as P

HD = 128
BLK = 128

SEQ = ("sy", "sc")
FSDP = ("fz", "fx")


def rotate_keys(key_heads, positions):
    half = key_heads.shape[-1] // 2
    freqs = jnp.exp(
        -jnp.arange(half, dtype=jnp.float32)
        * (2.0 / key_heads.shape[-1])
        * jnp.log(jnp.float32(1000000.0))
    )
    angle = positions.astype(jnp.float32)[:, None] * freqs[None, :]
    cosine = jnp.cos(angle)[:, None, :]
    sine = jnp.sin(angle)[:, None, :]
    first = key_heads[..., :half]
    second = key_heads[..., half:]
    return jnp.concatenate(
        [first * cosine - second * sine, second * cosine + first * sine], axis=-1
    )


def lookup_docs(token_index, block_table):
    block_index = token_index // BLK
    matches = block_index[:, None] == jnp.arange(block_table.shape[0], dtype=jnp.int32)[None, :]
    return jnp.sum(jnp.where(matches, block_table[None, :], 0), axis=1)


def doc_positions(token_index, doc_starts, block_docs):
    docs = lookup_docs(token_index, block_docs[0])
    doc_match = docs[:, None] == jnp.arange(doc_starts.shape[1], dtype=jnp.int32)[None, :]
    doc_first = jnp.sum(jnp.where(doc_match, doc_starts[0][None, :], 0), axis=1)
    return docs, token_index - doc_first


def shift(x, axis, size, step):
    return lax.ppermute(x, axis, [(i, (i + step) % size) for i in range(size)])


def ring_pieces(piece, axis, size):
    half = piece.shape[1] // 2
    from_prev = shift(piece, axis, size, 1)
    from_next = shift(piece, axis, size, -1)
    far_head = shift(from_prev[:, :half], axis, size, 1)
    far_tail = shift(from_next[:, half:], axis, size, -1)
    return [(-1, 0, from_prev), (1, 0, from_next), (2, 0, far_head), (2, half, far_tail)]


def gather_rows(w_part):
    nz = lax.axis_size("fz")
    nx = lax.axis_size("fx")
    fz = lax.axis_index("fz")
    fx = lax.axis_index("fx")
    rows = w_part.shape[1]
    full = jnp.zeros((w_part.shape[0], rows * nz * nx, w_part.shape[2]), w_part.dtype)

    def place(buf, part, z, x, sub):
        start = ((z % nz) * nx + (x % nx)) * rows + sub
        return lax.dynamic_update_slice(buf, part, (0, start, 0))

    def x_ring(buf, part, z, sub):
        buf = place(buf, part, z, fx, sub)
        for dx, sub2, got in ring_pieces(part, "fx", nx):
            buf = place(buf, got, z, fx + dx, sub + sub2)
        return buf

    full = x_ring(full, w_part, fz, 0)
    for dz, sub, got in ring_pieces(w_part, "fz", nz):
        full = x_ring(full, got, fz + dz, sub)
    return full


def make_per_device(cores):
    def per_device(hidden, queries, w_kv, b_kv, doc_starts, block_docs):
        tok_count = hidden.shape[1]
        core = lax.axis_index("sc")
        chip = lax.axis_index("sy")
        cols = w_kv.shape[2] // cores
        w_part = lax.dynamic_slice_in_dim(w_kv, core * cols, cols, axis=2)
        b_part = lax.dynamic_slice_in_dim(b_kv, core * cols, cols, axis=1)
        own_rows = hidden[0]
        partner_rows = lax.ppermute(own_rows, "sc", [(i, (i + 1) % cores) for i in range(cores)])
        chip_rows = jnp.where(
            core == 0,
            jnp.concatenate([own_rows, partner_rows]),
            jnp.concatenate([partner_rows, own_rows]),
        )
        chip_tokens = chip_rows.shape[0]
        key_value = jnp.einsum(
            "td,cde->cte",
            chip_rows,
            gather_rows(w_part),
            preferred_element_type=jnp.float32,
        )
        key_value = key_value + b_part.astype(jnp.float32)[:, None, :]
        chip_pos = chip * chip_tokens + jnp.arange(chip_tokens, dtype=jnp.int32)
        _, positions = doc_positions(chip_pos, doc_starts, block_docs)
        part_heads = cols // HD
        rotated = rotate_keys(key_value[0].reshape(chip_tokens, part_heads, HD), positions)
        keys = rotated.astype(jnp.bfloat16).reshape(chip_tokens, cols)
        values = key_value[1].astype(jnp.bfloat16)
        stacked = jnp.stack([keys, values])
        gathered = lax.all_gather(stacked, SEQ, axis=0, tiled=False)
        chips = gathered.shape[0] // cores
        gathered = gathered.reshape(chips, cores, 2, chip_tokens, cols)
        piece = jnp.transpose(gathered, (2, 0, 3, 1, 4)).reshape(2, chips * chip_tokens, cores * cols)

        seq_pos = (chip * cores + core) * tok_count + jnp.arange(tok_count, dtype=jnp.int32)
        query_docs = lookup_docs(seq_pos, block_docs[0])
        key_heads = piece.shape[2] // HD
        group = queries.shape[2] // HD // key_heads
        query_heads = queries[0].reshape(tok_count, key_heads, group, HD)
        inv_root = 1.0 / jnp.sqrt(jnp.float32(HD))
        width = piece.shape[1]
        key_docs = lookup_docs(jnp.arange(width, dtype=jnp.int32), block_docs[0])
        same_doc = query_docs[:, None] == key_docs[None, :]
        run_max = jnp.full((key_heads, group, tok_count), -1e30, jnp.float32)
        key_part = piece[0].reshape(width, key_heads, HD)
        value_part = piece[1].reshape(width, key_heads, HD)
        scores = (
            jnp.einsum("tgjd,sgd->gjts", query_heads, key_part, preferred_element_type=jnp.float32)
            * inv_root
        )
        scores = jnp.where(same_doc[None, None], scores, jnp.float32(-1e30))
        new_max = jnp.maximum(run_max, jnp.max(scores, axis=-1))
        weight = jnp.where(same_doc[None, None], jnp.exp(scores - new_max[..., None]), jnp.float32(0.0))
        new_sum = jnp.sum(weight, axis=-1)
        update = jnp.einsum(
            "gjts,sgd->gjtd",
            weight.astype(jnp.bfloat16),
            value_part,
            preferred_element_type=jnp.float32,
        )
        result = update / new_sum[..., None]
        result = jnp.transpose(result, (2, 0, 1, 3)).reshape(tok_count, key_heads * group * HD)
        return result.astype(jnp.bfloat16)[None]

    return per_device


def solution(mesh):
    seq, fsdp, tp = (mesh.shape[name] for name in ("seq", "fsdp", "tp"))
    cores = 2
    x_size = 4
    fine = Mesh(
        mesh.devices.reshape(seq // cores, cores, fsdp // x_size, x_size, tp),
        ("sy", "sc", "fz", "fx", "tp"),
    )
    in_specs = (
        P(FSDP, SEQ, None),
        P(FSDP, SEQ, "tp"),
        P(None, FSDP, "tp"),
        P(None, "tp"),
        P(FSDP, None),
        P(FSDP, None),
    )
    out_specs = P(FSDP, SEQ, "tp")
    return jax.shard_map(
        make_per_device(cores), mesh=fine, in_specs=in_specs, out_specs=out_specs, check_vma=False
    )
```

```python
import jax
import jax.numpy as jnp
from jax import lax
from jax.sharding import Mesh
from jax.sharding import PartitionSpec as P

HD = 128
BLK = 128

SEQ = ("sy", "sc")
FSDP = ("fz", "fx")


def rotate_keys(key_heads, positions):
    half = key_heads.shape[-1] // 2
    freqs = jnp.exp(
        -jnp.arange(half, dtype=jnp.float32)
        * (2.0 / key_heads.shape[-1])
        * jnp.log(jnp.float32(1000000.0))
    )
    angle = positions.astype(jnp.float32)[:, None] * freqs[None, :]
    cosine = jnp.cos(angle)[:, None, :]
    sine = jnp.sin(angle)[:, None, :]
    first = key_heads[..., :half]
    second = key_heads[..., half:]
    return jnp.concatenate(
        [first * cosine - second * sine, second * cosine + first * sine], axis=-1
    )


def lookup_docs(token_index, block_table):
    block_index = token_index // BLK
    matches = block_index[:, None] == jnp.arange(block_table.shape[0], dtype=jnp.int32)[None, :]
    return jnp.sum(jnp.where(matches, block_table[None, :], 0), axis=1)


def doc_positions(token_index, doc_starts, block_docs):
    docs = lookup_docs(token_index, block_docs[0])
    doc_match = docs[:, None] == jnp.arange(doc_starts.shape[1], dtype=jnp.int32)[None, :]
    doc_first = jnp.sum(jnp.where(doc_match, doc_starts[0][None, :], 0), axis=1)
    return docs, token_index - doc_first


def shift(x, axis, size, step):
    return lax.ppermute(x, axis, [(i, (i + step) % size) for i in range(size)])


def ring_gather(piece, axis, size):
    half = piece.shape[-1] // 2
    from_prev = shift(piece, axis, size, 1)
    from_next = shift(piece, axis, size, -1)
    far_head = shift(from_prev[..., :half], axis, size, 1)
    far_tail = shift(from_next[..., half:], axis, size, -1)
    return jnp.concatenate([piece, from_next, far_head, far_tail, from_prev], axis=-1)


def gather_rows(w_part):
    nz = lax.axis_size("fz")
    nx = lax.axis_size("fx")
    fz = lax.axis_index("fz")
    fx = lax.axis_index("fx")
    split = w_part.shape[1] // 2
    by_sc = lax.all_gather(w_part[:, :split], FSDP, axis=2, tiled=True)
    rel = ring_gather(ring_gather(w_part[:, split:], "fz", nz), "fx", nx)
    c, e, rows = rel.shape[0], rel.shape[1], rel.shape[2] // (nz * nx)
    rel = rel.reshape(c, e, nx, nz, rows)
    rel = jnp.roll(rel, (fx, fz), axis=(2, 3))
    by_pp = jnp.swapaxes(rel, 2, 3).reshape(c, e, nz * nx * rows)
    return jnp.concatenate([by_sc, by_pp], axis=1)


def make_per_device(cores):
    def per_device(hidden, queries, w_kv, b_kv, doc_starts, block_docs):
        tok_count = hidden.shape[1]
        core = lax.axis_index("sc")
        chip = lax.axis_index("sy")
        cols = w_kv.shape[2] // cores
        w_part = lax.dynamic_slice_in_dim(w_kv, core * cols, cols, axis=2)
        b_part = lax.dynamic_slice_in_dim(b_kv, core * cols, cols, axis=1)
        own_rows = hidden[0]
        partner_rows = lax.ppermute(own_rows, "sc", [(i, (i + 1) % cores) for i in range(cores)])
        chip_rows = jnp.where(
            core == 0,
            jnp.concatenate([own_rows, partner_rows]),
            jnp.concatenate([partner_rows, own_rows]),
        )
        chip_tokens = chip_rows.shape[0]
        key_value = jnp.einsum(
            "td,ced->cte",
            chip_rows,
            gather_rows(jnp.swapaxes(w_part, 1, 2)),
            preferred_element_type=jnp.float32,
        )
        key_value = key_value + b_part.astype(jnp.float32)[:, None, :]
        chip_pos = chip * chip_tokens + jnp.arange(chip_tokens, dtype=jnp.int32)
        _, positions = doc_positions(chip_pos, doc_starts, block_docs)
        part_heads = cols // HD
        rotated = rotate_keys(key_value[0].reshape(chip_tokens, part_heads, HD), positions)
        keys = rotated.astype(jnp.bfloat16).reshape(chip_tokens, cols)
        values = key_value[1].astype(jnp.bfloat16)
        stacked = jnp.stack([keys, values])
        gathered = lax.all_gather(stacked, SEQ, axis=0, tiled=False)
        chips = gathered.shape[0] // cores
        gathered = gathered.reshape(chips, cores, 2, chip_tokens, cols)
        piece = jnp.transpose(gathered, (2, 0, 3, 1, 4)).reshape(2, chips * chip_tokens, cores * cols)

        seq_pos = (chip * cores + core) * tok_count + jnp.arange(tok_count, dtype=jnp.int32)
        query_docs = lookup_docs(seq_pos, block_docs[0])
        key_heads = piece.shape[2] // HD
        group = queries.shape[2] // HD // key_heads
        query_heads = queries[0].reshape(tok_count, key_heads, group, HD)
        inv_root = 1.0 / jnp.sqrt(jnp.float32(HD))
        width = piece.shape[1]
        key_docs = lookup_docs(jnp.arange(width, dtype=jnp.int32), block_docs[0])
        same_doc = query_docs[:, None] == key_docs[None, :]
        run_max = jnp.full((key_heads, group, tok_count), -1e30, jnp.float32)
        key_part = piece[0].reshape(width, key_heads, HD)
        value_part = piece[1].reshape(width, key_heads, HD)
        scores = (
            jnp.einsum("tgjd,sgd->gjts", query_heads, key_part, preferred_element_type=jnp.float32)
            * inv_root
        )
        scores = jnp.where(same_doc[None, None], scores, jnp.float32(-1e30))
        new_max = jnp.maximum(run_max, jnp.max(scores, axis=-1))
        weight = jnp.where(same_doc[None, None], jnp.exp(scores - new_max[..., None]), jnp.float32(0.0))
        new_sum = jnp.sum(weight, axis=-1)
        update = jnp.einsum(
            "gjts,sgd->gjtd",
            weight.astype(jnp.bfloat16),
            value_part,
            preferred_element_type=jnp.float32,
        )
        result = update / new_sum[..., None]
        result = jnp.transpose(result, (2, 0, 1, 3)).reshape(tok_count, key_heads * group * HD)
        return result.astype(jnp.bfloat16)[None]

    return per_device


def solution(mesh):
    seq, fsdp, tp = (mesh.shape[name] for name in ("seq", "fsdp", "tp"))
    cores = 2
    x_size = 4
    fine = Mesh(
        mesh.devices.reshape(seq // cores, cores, fsdp // x_size, x_size, tp),
        ("sy", "sc", "fz", "fx", "tp"),
    )
    in_specs = (
        P(FSDP, SEQ, None),
        P(FSDP, SEQ, "tp"),
        P(None, FSDP, "tp"),
        P(None, "tp"),
        P(FSDP, None),
        P(FSDP, None),
    )
    out_specs = P(FSDP, SEQ, "tp")
    return jax.shard_map(
        make_per_device(cores), mesh=fine, in_specs=in_specs, out_specs=out_specs, check_vma=False
    )
```

```python
import jax
import jax.numpy as jnp
from jax import lax
from jax.sharding import Mesh
from jax.sharding import PartitionSpec as P

HD = 128
BLK = 128

SEQ = ("sy", "sc")
FSDP = ("fz", "fx")


def rotate_keys(key_heads, positions):
    half = key_heads.shape[-1] // 2
    freqs = jnp.exp(
        -jnp.arange(half, dtype=jnp.float32)
        * (2.0 / key_heads.shape[-1])
        * jnp.log(jnp.float32(1000000.0))
    )
    angle = positions.astype(jnp.float32)[:, None] * freqs[None, :]
    cosine = jnp.cos(angle)[:, None, :]
    sine = jnp.sin(angle)[:, None, :]
    first = key_heads[..., :half]
    second = key_heads[..., half:]
    return jnp.concatenate(
        [first * cosine - second * sine, second * cosine + first * sine], axis=-1
    )


def lookup_docs(token_index, block_table):
    block_index = token_index // BLK
    matches = block_index[:, None] == jnp.arange(block_table.shape[0], dtype=jnp.int32)[None, :]
    return jnp.sum(jnp.where(matches, block_table[None, :], 0), axis=1)


def doc_positions(token_index, doc_starts, block_docs):
    docs = lookup_docs(token_index, block_docs[0])
    doc_match = docs[:, None] == jnp.arange(doc_starts.shape[1], dtype=jnp.int32)[None, :]
    doc_first = jnp.sum(jnp.where(doc_match, doc_starts[0][None, :], 0), axis=1)
    return docs, token_index - doc_first


def shift(x, axis, size, step):
    return lax.ppermute(x, axis, [(i, (i + step) % size) for i in range(size)])


def ring_gather(piece, axis, size, dim):
    half = piece.shape[dim] // 2
    from_prev = shift(piece, axis, size, 1)
    from_next = shift(piece, axis, size, -1)
    far_head = shift(lax.slice_in_dim(from_prev, 0, half, axis=dim), axis, size, 1)
    far_tail = shift(lax.slice_in_dim(from_next, half, 2 * half, axis=dim), axis, size, -1)
    return jnp.concatenate([piece, from_next, far_head, far_tail, from_prev], axis=dim)


def swap_partner(x, cores, dim):
    core = lax.axis_index("sc")
    other = lax.ppermute(x, "sc", [(i, (i + 1) % cores) for i in range(cores)])
    return jnp.where(
        core == 0,
        jnp.concatenate([x, other], axis=dim),
        jnp.concatenate([other, x], axis=dim),
    )


def make_per_device(cores):
    def per_device(hidden, queries, w_kv, b_kv, doc_starts, block_docs):
        tok_count = hidden.shape[1]
        core = lax.axis_index("sc")
        chip = lax.axis_index("sy")
        nz, nx, ny = lax.axis_size("fz"), lax.axis_size("fx"), lax.axis_size("sy")
        fz, fx = lax.axis_index("fz"), lax.axis_index("fx")
        cols = w_kv.shape[2] // cores
        w_part = jnp.swapaxes(lax.dynamic_slice_in_dim(w_kv, core * cols, cols, axis=2), 1, 2)
        b_part = lax.dynamic_slice_in_dim(b_kv, core * cols, cols, axis=1)
        chip_rows = swap_partner(hidden[0], cores, 0)
        chip_tokens = chip_rows.shape[0]
        split = cols // 2
        w_sc = lax.all_gather(w_part[:, :split], FSDP, axis=2, tiled=True)
        w_ring = ring_gather(ring_gather(w_part[:, split:], "fz", nz, 2), "fx", nx, 2)
        blocks = nz * nx
        rows = w_part.shape[2]
        ring_pos = jnp.arange(blocks, dtype=jnp.int32)
        ring_block = ((fz + ring_pos % nz) % nz) * nx + (fx + ring_pos // nz) % nx
        pick = (jnp.arange(blocks, dtype=jnp.int32)[:, None] == ring_block[None, :]).astype(chip_rows.dtype)
        ring_rows = jnp.einsum(
            "tbd,bp->tpd",
            chip_rows.reshape(chip_tokens, blocks, rows),
            pick,
            preferred_element_type=jnp.float32,
        ).astype(chip_rows.dtype).reshape(chip_tokens, blocks * rows)
        kv_sc = jnp.einsum("td,ced->cte", chip_rows, w_sc, preferred_element_type=jnp.float32)
        kv_ring = jnp.einsum("td,ced->cte", ring_rows, w_ring, preferred_element_type=jnp.float32)
        key_value = jnp.concatenate([kv_sc, kv_ring], axis=2)
        key_value = key_value + b_part.astype(jnp.float32)[:, None, :]
        chip_pos = chip * chip_tokens + jnp.arange(chip_tokens, dtype=jnp.int32)
        _, positions = doc_positions(chip_pos, doc_starts, block_docs)
        part_heads = cols // HD
        rotated = rotate_keys(key_value[0].reshape(chip_tokens, part_heads, HD), positions)
        keys = rotated.astype(jnp.bfloat16).reshape(chip_tokens, cols)
        values = key_value[1].astype(jnp.bfloat16)
        stacked = jnp.stack([keys, values])
        piece = swap_partner(ring_gather(stacked, "sy", ny, 1), cores, 2)
        width = piece.shape[1]
        ring_tok = jnp.arange(width, dtype=jnp.int32)
        key_tokens = ((chip + ring_tok // chip_tokens) % ny) * chip_tokens + ring_tok % chip_tokens

        seq_pos = (chip * cores + core) * tok_count + jnp.arange(tok_count, dtype=jnp.int32)
        query_docs = lookup_docs(seq_pos, block_docs[0])
        key_heads = piece.shape[2] // HD
        group = queries.shape[2] // HD // key_heads
        query_heads = queries[0].reshape(tok_count, key_heads, group, HD)
        inv_root = 1.0 / jnp.sqrt(jnp.float32(HD))
        key_docs = lookup_docs(key_tokens, block_docs[0])
        same_doc = query_docs[:, None] == key_docs[None, :]
        run_max = jnp.full((key_heads, group, tok_count), -1e30, jnp.float32)
        key_part = piece[0].reshape(width, key_heads, HD)
        value_part = piece[1].reshape(width, key_heads, HD)
        scores = (
            jnp.einsum("tgjd,sgd->gjts", query_heads, key_part, preferred_element_type=jnp.float32)
            * inv_root
        )
        scores = jnp.where(same_doc[None, None], scores, jnp.float32(-1e30))
        new_max = jnp.maximum(run_max, jnp.max(scores, axis=-1))
        weight = jnp.where(same_doc[None, None], jnp.exp(scores - new_max[..., None]), jnp.float32(0.0))
        new_sum = jnp.sum(weight, axis=-1)
        update = jnp.einsum(
            "gjts,sgd->gjtd",
            weight.astype(jnp.bfloat16),
            value_part,
            preferred_element_type=jnp.float32,
        )
        result = update / new_sum[..., None]
        result = jnp.transpose(result, (2, 0, 1, 3)).reshape(tok_count, key_heads * group * HD)
        return result.astype(jnp.bfloat16)[None]

    return per_device


def solution(mesh):
    seq, fsdp, tp = (mesh.shape[name] for name in ("seq", "fsdp", "tp"))
    cores = 2
    x_size = 4
    fine = Mesh(
        mesh.devices.reshape(seq // cores, cores, fsdp // x_size, x_size, tp),
        ("sy", "sc", "fz", "fx", "tp"),
    )
    in_specs = (
        P(FSDP, SEQ, None),
        P(FSDP, SEQ, "tp"),
        P(None, FSDP, "tp"),
        P(None, "tp"),
        P(FSDP, None),
        P(FSDP, None),
    )
    out_specs = P(FSDP, SEQ, "tp")
    return jax.shard_map(
        make_per_device(cores), mesh=fine, in_specs=in_specs, out_specs=out_specs, check_vma=False
    )
```

```python
import jax
import jax.numpy as jnp
from jax import lax
from jax.sharding import Mesh
from jax.sharding import PartitionSpec as P

HD = 128
BLK = 128

SEQ = ("sy", "sc")
FSDP = ("fz", "fx")


def rotate_keys(key_heads, positions):
    half = key_heads.shape[-1] // 2
    freqs = jnp.exp(
        -jnp.arange(half, dtype=jnp.float32)
        * (2.0 / key_heads.shape[-1])
        * jnp.log(jnp.float32(1000000.0))
    )
    angle = positions.astype(jnp.float32)[:, None] * freqs[None, :]
    cosine = jnp.cos(angle)[:, None, :]
    sine = jnp.sin(angle)[:, None, :]
    first = key_heads[..., :half]
    second = key_heads[..., half:]
    return jnp.concatenate(
        [first * cosine - second * sine, second * cosine + first * sine], axis=-1
    )


def lookup_docs(token_index, block_table):
    block_index = token_index // BLK
    matches = block_index[:, None] == jnp.arange(block_table.shape[0], dtype=jnp.int32)[None, :]
    return jnp.sum(jnp.where(matches, block_table[None, :], 0), axis=1)


def doc_positions(token_index, doc_starts, block_docs):
    docs = lookup_docs(token_index, block_docs[0])
    doc_match = docs[:, None] == jnp.arange(doc_starts.shape[1], dtype=jnp.int32)[None, :]
    doc_first = jnp.sum(jnp.where(doc_match, doc_starts[0][None, :], 0), axis=1)
    return docs, token_index - doc_first


def shift(x, axis, size, step):
    return lax.ppermute(x, axis, [(i, (i + step) % size) for i in range(size)])


def ring_gather(piece, axis, size, dim):
    half = piece.shape[dim] // 2
    from_prev = shift(piece, axis, size, 1)
    from_next = shift(piece, axis, size, -1)
    far_head = shift(lax.slice_in_dim(from_prev, 0, half, axis=dim), axis, size, 1)
    far_tail = shift(lax.slice_in_dim(from_next, half, 2 * half, axis=dim), axis, size, -1)
    return jnp.concatenate([piece, from_next, far_head, far_tail, from_prev], axis=dim)


def swap_partner(x, cores, dim):
    core = lax.axis_index("sc")
    other = lax.ppermute(x, "sc", [(i, (i + 1) % cores) for i in range(cores)])
    return jnp.where(
        core == 0,
        jnp.concatenate([x, other], axis=dim),
        jnp.concatenate([other, x], axis=dim),
    )


def make_per_device(cores):
    def per_device(hidden, queries, w_kv, b_kv, doc_starts, block_docs):
        tok_count = hidden.shape[1]
        core = lax.axis_index("sc")
        chip = lax.axis_index("sy")
        nz, nx, ny = lax.axis_size("fz"), lax.axis_size("fx"), lax.axis_size("sy")
        fz, fx = lax.axis_index("fz"), lax.axis_index("fx")
        cols = w_kv.shape[2] // cores
        w_part = jnp.swapaxes(lax.dynamic_slice_in_dim(w_kv, core * cols, cols, axis=2), 1, 2)
        b_part = lax.dynamic_slice_in_dim(b_kv, core * cols, cols, axis=1)
        chip_rows = swap_partner(hidden[0], cores, 0)
        chip_tokens = chip_rows.shape[0]
        split = cols // 2
        w_sc = lax.all_gather(w_part[:, :split], FSDP, axis=2, tiled=True)
        blocks = nz * nx
        rows = w_part.shape[2]
        ring_pos = jnp.arange(blocks, dtype=jnp.int32)
        ring_block = ((fz + ring_pos % nz) % nz) * nx + (fx + ring_pos // nz) % nx
        pick = (jnp.arange(blocks, dtype=jnp.int32)[:, None] == ring_block[None, :]).astype(chip_rows.dtype)
        ring_rows = jnp.einsum(
            "tbd,bp->tpd",
            chip_rows.reshape(chip_tokens, blocks, rows),
            pick,
            preferred_element_type=jnp.float32,
        ).astype(chip_rows.dtype).reshape(chip_tokens, blocks * rows)
        z_ring, ring_rows = lax.optimization_barrier(
            (ring_gather(w_part[:, split:], "fz", nz, 2), ring_rows)
        )
        w_ring = ring_gather(z_ring, "fx", nx, 2)
        kv_sc = jnp.einsum("td,ced->cte", chip_rows, w_sc, preferred_element_type=jnp.float32)
        kv_ring = jnp.einsum("td,ced->cte", ring_rows, w_ring, preferred_element_type=jnp.float32)
        key_value = jnp.concatenate([kv_sc, kv_ring], axis=2)
        key_value = key_value + b_part.astype(jnp.float32)[:, None, :]
        chip_pos = chip * chip_tokens + jnp.arange(chip_tokens, dtype=jnp.int32)
        _, positions = doc_positions(chip_pos, doc_starts, block_docs)
        part_heads = cols // HD
        rotated = rotate_keys(key_value[0].reshape(chip_tokens, part_heads, HD), positions)
        keys = rotated.astype(jnp.bfloat16).reshape(chip_tokens, cols)
        values = key_value[1].astype(jnp.bfloat16)
        stacked = jnp.stack([keys, values])
        piece = swap_partner(ring_gather(stacked, "sy", ny, 1), cores, 2)
        width = piece.shape[1]
        ring_tok = jnp.arange(width, dtype=jnp.int32)
        key_tokens = ((chip + ring_tok // chip_tokens) % ny) * chip_tokens + ring_tok % chip_tokens

        seq_pos = (chip * cores + core) * tok_count + jnp.arange(tok_count, dtype=jnp.int32)
        query_docs = lookup_docs(seq_pos, block_docs[0])
        key_heads = piece.shape[2] // HD
        group = queries.shape[2] // HD // key_heads
        query_heads = queries[0].reshape(tok_count, key_heads, group, HD)
        inv_root = 1.0 / jnp.sqrt(jnp.float32(HD))
        key_docs = lookup_docs(key_tokens, block_docs[0])
        same_doc = query_docs[:, None] == key_docs[None, :]
        run_max = jnp.full((key_heads, group, tok_count), -1e30, jnp.float32)
        key_part = piece[0].reshape(width, key_heads, HD)
        value_part = piece[1].reshape(width, key_heads, HD)
        scores = (
            jnp.einsum("tgjd,sgd->gjts", query_heads, key_part, preferred_element_type=jnp.float32)
            * inv_root
        )
        scores = jnp.where(same_doc[None, None], scores, jnp.float32(-1e30))
        new_max = jnp.maximum(run_max, jnp.max(scores, axis=-1))
        weight = jnp.where(same_doc[None, None], jnp.exp(scores - new_max[..., None]), jnp.float32(0.0))
        new_sum = jnp.sum(weight, axis=-1)
        update = jnp.einsum(
            "gjts,sgd->gjtd",
            weight.astype(jnp.bfloat16),
            value_part,
            preferred_element_type=jnp.float32,
        )
        result = update / new_sum[..., None]
        result = jnp.transpose(result, (2, 0, 1, 3)).reshape(tok_count, key_heads * group * HD)
        return result.astype(jnp.bfloat16)[None]

    return per_device


def solution(mesh):
    seq, fsdp, tp = (mesh.shape[name] for name in ("seq", "fsdp", "tp"))
    cores = 2
    x_size = 4
    fine = Mesh(
        mesh.devices.reshape(seq // cores, cores, fsdp // x_size, x_size, tp),
        ("sy", "sc", "fz", "fx", "tp"),
    )
    in_specs = (
        P(FSDP, SEQ, None),
        P(FSDP, SEQ, "tp"),
        P(None, FSDP, "tp"),
        P(None, "tp"),
        P(FSDP, None),
        P(FSDP, None),
    )
    out_specs = P(FSDP, SEQ, "tp")
    return jax.shard_map(
        make_per_device(cores), mesh=fine, in_specs=in_specs, out_specs=out_specs, check_vma=False
    )
```

```python
import jax
import jax.numpy as jnp
from jax import lax
from jax.sharding import Mesh
from jax.sharding import PartitionSpec as P

HD = 128
BLK = 128

SEQ = ("sy", "sc")
FSDP = ("fz", "fx")


def rotate_keys(key_heads, positions):
    half = key_heads.shape[-1] // 2
    freqs = jnp.exp(
        -jnp.arange(half, dtype=jnp.float32)
        * (2.0 / key_heads.shape[-1])
        * jnp.log(jnp.float32(1000000.0))
    )
    angle = positions.astype(jnp.float32)[:, None] * freqs[None, :]
    cosine = jnp.cos(angle)[:, None, :]
    sine = jnp.sin(angle)[:, None, :]
    first = key_heads[..., :half]
    second = key_heads[..., half:]
    return jnp.concatenate(
        [first * cosine - second * sine, second * cosine + first * sine], axis=-1
    )


def lookup_docs(token_index, block_table):
    block_index = token_index // BLK
    matches = block_index[:, None] == jnp.arange(block_table.shape[0], dtype=jnp.int32)[None, :]
    return jnp.sum(jnp.where(matches, block_table[None, :], 0), axis=1)


def doc_positions(token_index, doc_starts, block_docs):
    docs = lookup_docs(token_index, block_docs[0])
    doc_match = docs[:, None] == jnp.arange(doc_starts.shape[1], dtype=jnp.int32)[None, :]
    doc_first = jnp.sum(jnp.where(doc_match, doc_starts[0][None, :], 0), axis=1)
    return docs, token_index - doc_first


def shift(x, axis, size, step):
    return lax.ppermute(x, axis, [(i, (i + step) % size) for i in range(size)])


def ring_gather(piece, axis, size, dim, tie=None):
    half = piece.shape[dim] // 2
    from_prev = shift(piece, axis, size, 1)
    from_next = shift(piece, axis, size, -1)
    if tie is not None:
        from_prev, from_next, tie = lax.optimization_barrier((from_prev, from_next, tie))
    far_head = shift(lax.slice_in_dim(from_prev, 0, half, axis=dim), axis, size, 1)
    far_tail = shift(lax.slice_in_dim(from_next, half, 2 * half, axis=dim), axis, size, -1)
    out = jnp.concatenate([piece, from_next, far_head, far_tail, from_prev], axis=dim)
    return out if tie is None else (out, tie)


def swap_partner(x, cores, dim):
    core = lax.axis_index("sc")
    other = lax.ppermute(x, "sc", [(i, (i + 1) % cores) for i in range(cores)])
    return jnp.where(
        core == 0,
        jnp.concatenate([x, other], axis=dim),
        jnp.concatenate([other, x], axis=dim),
    )


def make_per_device(cores):
    def per_device(hidden, queries, w_kv, b_kv, doc_starts, block_docs):
        tok_count = hidden.shape[1]
        core = lax.axis_index("sc")
        chip = lax.axis_index("sy")
        nz, nx, ny = lax.axis_size("fz"), lax.axis_size("fx"), lax.axis_size("sy")
        fz, fx = lax.axis_index("fz"), lax.axis_index("fx")
        cols = w_kv.shape[2] // cores
        w_part = jnp.swapaxes(lax.dynamic_slice_in_dim(w_kv, core * cols, cols, axis=2), 1, 2)
        b_part = lax.dynamic_slice_in_dim(b_kv, core * cols, cols, axis=1)
        chip_rows = swap_partner(hidden[0], cores, 0)
        chip_tokens = chip_rows.shape[0]
        split = cols // 2
        w_sc = lax.all_gather(w_part[:, :split], FSDP, axis=2, tiled=True)
        blocks = nz * nx
        rows = w_part.shape[2]
        z_ring = ring_gather(w_part[:, split:], "fz", nz, 2)
        z_block = lax.dynamic_slice_in_dim(z_ring, chip * rows, rows, axis=2)
        x_ring = ring_gather(z_block, "fx", nx, 2)
        ring_pos = jnp.arange(blocks, dtype=jnp.int32)
        ring_z = (fz + chip + ring_pos // nx) % nz
        ring_block = ring_z * nx + (fx + ring_pos % nx) % nx
        pick = (jnp.arange(blocks, dtype=jnp.int32)[:, None] == ring_block[None, :]).astype(chip_rows.dtype)
        ring_rows = jnp.einsum(
            "tbd,bp->tpd",
            chip_rows.reshape(chip_tokens, blocks, rows),
            pick,
            preferred_element_type=jnp.float32,
        ).astype(chip_rows.dtype).reshape(chip_tokens, blocks * rows)
        w_ring, ring_rows = ring_gather(x_ring, "sy", ny, 2, tie=ring_rows)
        kv_sc = jnp.einsum("td,ced->cte", chip_rows, w_sc, preferred_element_type=jnp.float32)
        kv_ring = jnp.einsum("td,ced->cte", ring_rows, w_ring, preferred_element_type=jnp.float32)
        key_value = jnp.concatenate([kv_sc, kv_ring], axis=2)
        key_value = key_value + b_part.astype(jnp.float32)[:, None, :]
        chip_pos = chip * chip_tokens + jnp.arange(chip_tokens, dtype=jnp.int32)
        _, positions = doc_positions(chip_pos, doc_starts, block_docs)
        part_heads = cols // HD
        rotated = rotate_keys(key_value[0].reshape(chip_tokens, part_heads, HD), positions)
        keys = rotated.astype(jnp.bfloat16).reshape(chip_tokens, cols)
        values = key_value[1].astype(jnp.bfloat16)
        stacked = jnp.stack([keys, values])
        piece = swap_partner(ring_gather(stacked, "sy", ny, 1), cores, 2)
        width = piece.shape[1]
        ring_tok = jnp.arange(width, dtype=jnp.int32)
        key_tokens = ((chip + ring_tok // chip_tokens) % ny) * chip_tokens + ring_tok % chip_tokens

        seq_pos = (chip * cores + core) * tok_count + jnp.arange(tok_count, dtype=jnp.int32)
        query_docs = lookup_docs(seq_pos, block_docs[0])
        key_heads = piece.shape[2] // HD
        group = queries.shape[2] // HD // key_heads
        query_heads = queries[0].reshape(tok_count, key_heads, group, HD)
        inv_root = 1.0 / jnp.sqrt(jnp.float32(HD))
        key_docs = lookup_docs(key_tokens, block_docs[0])
        same_doc = query_docs[:, None] == key_docs[None, :]
        run_max = jnp.full((key_heads, group, tok_count), -1e30, jnp.float32)
        key_part = piece[0].reshape(width, key_heads, HD)
        value_part = piece[1].reshape(width, key_heads, HD)
        scores = (
            jnp.einsum("tgjd,sgd->gjts", query_heads, key_part, preferred_element_type=jnp.float32)
            * inv_root
        )
        scores = jnp.where(same_doc[None, None], scores, jnp.float32(-1e30))
        new_max = jnp.maximum(run_max, jnp.max(scores, axis=-1))
        weight = jnp.where(same_doc[None, None], jnp.exp(scores - new_max[..., None]), jnp.float32(0.0))
        new_sum = jnp.sum(weight, axis=-1)
        update = jnp.einsum(
            "gjts,sgd->gjtd",
            weight.astype(jnp.bfloat16),
            value_part,
            preferred_element_type=jnp.float32,
        )
        result = update / new_sum[..., None]
        result = jnp.transpose(result, (2, 0, 1, 3)).reshape(tok_count, key_heads * group * HD)
        return result.astype(jnp.bfloat16)[None]

    return per_device


def solution(mesh):
    seq, fsdp, tp = (mesh.shape[name] for name in ("seq", "fsdp", "tp"))
    cores = 2
    x_size = 4
    fine = Mesh(
        mesh.devices.reshape(seq // cores, cores, fsdp // x_size, x_size, tp),
        ("sy", "sc", "fz", "fx", "tp"),
    )
    in_specs = (
        P(FSDP, SEQ, None),
        P(FSDP, SEQ, "tp"),
        P(None, FSDP, "tp"),
        P(None, "tp"),
        P(FSDP, None),
        P(FSDP, None),
    )
    out_specs = P(FSDP, SEQ, "tp")
    return jax.shard_map(
        make_per_device(cores), mesh=fine, in_specs=in_specs, out_specs=out_specs, check_vma=False
    )
```

```python
import jax
import jax.numpy as jnp
from jax import lax
from jax.sharding import Mesh
from jax.sharding import PartitionSpec as P

HD = 128
BLK = 128

SEQ = ("sy", "sc")
FSDP = ("fz", "fx")


def rotate_keys(key_heads, positions):
    half = key_heads.shape[-1] // 2
    freqs = jnp.exp(
        -jnp.arange(half, dtype=jnp.float32)
        * (2.0 / key_heads.shape[-1])
        * jnp.log(jnp.float32(1000000.0))
    )
    angle = positions.astype(jnp.float32)[:, None] * freqs[None, :]
    cosine = jnp.cos(angle)[:, None, :]
    sine = jnp.sin(angle)[:, None, :]
    first = key_heads[..., :half]
    second = key_heads[..., half:]
    return jnp.concatenate(
        [first * cosine - second * sine, second * cosine + first * sine], axis=-1
    )


def lookup_docs(token_index, block_table):
    block_index = token_index // BLK
    matches = block_index[:, None] == jnp.arange(block_table.shape[0], dtype=jnp.int32)[None, :]
    return jnp.sum(jnp.where(matches, block_table[None, :], 0), axis=1)


def doc_positions(token_index, doc_starts, block_docs):
    docs = lookup_docs(token_index, block_docs[0])
    doc_match = docs[:, None] == jnp.arange(doc_starts.shape[1], dtype=jnp.int32)[None, :]
    doc_first = jnp.sum(jnp.where(doc_match, doc_starts[0][None, :], 0), axis=1)
    return docs, token_index - doc_first


def shift(x, axis, size, step):
    return lax.ppermute(x, axis, [(i, (i + step) % size) for i in range(size)])


def ring_gather(piece, axis, size, dim, tie=None):
    half = piece.shape[dim] // 2
    from_prev = shift(piece, axis, size, 1)
    from_next = shift(piece, axis, size, -1)
    if tie is not None:
        from_prev, from_next, tie = lax.optimization_barrier((from_prev, from_next, tie))
    far_head = shift(lax.slice_in_dim(from_prev, 0, half, axis=dim), axis, size, 1)
    far_tail = shift(lax.slice_in_dim(from_next, half, 2 * half, axis=dim), axis, size, -1)
    out = jnp.concatenate([piece, from_next, far_head, far_tail, from_prev], axis=dim)
    return out if tie is None else (out, tie)


def swap_partner(x, cores, dim):
    core = lax.axis_index("sc")
    other = lax.ppermute(x, "sc", [(i, (i + 1) % cores) for i in range(cores)])
    return jnp.where(
        core == 0,
        jnp.concatenate([x, other], axis=dim),
        jnp.concatenate([other, x], axis=dim),
    )


def make_per_device(cores):
    def per_device(hidden, queries, w_kv, b_kv, doc_starts, block_docs):
        tok_count = hidden.shape[1]
        core = lax.axis_index("sc")
        chip = lax.axis_index("sy")
        nz, nx, ny = lax.axis_size("fz"), lax.axis_size("fx"), lax.axis_size("sy")
        fz, fx = lax.axis_index("fz"), lax.axis_index("fx")
        cols = w_kv.shape[2] // cores
        w_part = jnp.swapaxes(lax.dynamic_slice_in_dim(w_kv, core * cols, cols, axis=2), 1, 2)
        b_part = lax.dynamic_slice_in_dim(b_kv, core * cols, cols, axis=1)
        chip_rows = swap_partner(hidden[0], cores, 0)
        chip_tokens = chip_rows.shape[0]
        split = cols // 2
        w_sc = lax.all_gather(w_part[:, :split], FSDP, axis=2, tiled=True)
        blocks = nz * nx
        rows = w_part.shape[2]
        own_block = w_part[:, split:]
        fetch = [
            (y * nz + (z + y) % nz, y * nz + z) for y in range(1, ny) for z in range(nz)
        ]
        fetched = lax.ppermute(own_block, ("sy", "fz"), fetch)
        z_block = jnp.where(chip == 0, own_block, fetched)
        x_ring = ring_gather(z_block, "fx", nx, 2)
        ring_pos = jnp.arange(blocks, dtype=jnp.int32)
        ring_z = (fz + chip + ring_pos // nx) % nz
        ring_block = ring_z * nx + (fx + ring_pos % nx) % nx
        pick = (jnp.arange(blocks, dtype=jnp.int32)[:, None] == ring_block[None, :]).astype(chip_rows.dtype)
        ring_rows = jnp.einsum(
            "tbd,bp->tpd",
            chip_rows.reshape(chip_tokens, blocks, rows),
            pick,
            preferred_element_type=jnp.float32,
        ).astype(chip_rows.dtype).reshape(chip_tokens, blocks * rows)
        w_ring, ring_rows = ring_gather(x_ring, "sy", ny, 2, tie=ring_rows)
        kv_sc = jnp.einsum("td,ced->cte", chip_rows, w_sc, preferred_element_type=jnp.float32)
        kv_ring = jnp.einsum("td,ced->cte", ring_rows, w_ring, preferred_element_type=jnp.float32)
        key_value = jnp.concatenate([kv_sc, kv_ring], axis=2)
        key_value = key_value + b_part.astype(jnp.float32)[:, None, :]
        chip_pos = chip * chip_tokens + jnp.arange(chip_tokens, dtype=jnp.int32)
        _, positions = doc_positions(chip_pos, doc_starts, block_docs)
        part_heads = cols // HD
        rotated = rotate_keys(key_value[0].reshape(chip_tokens, part_heads, HD), positions)
        keys = rotated.astype(jnp.bfloat16).reshape(chip_tokens, cols)
        values = key_value[1].astype(jnp.bfloat16)
        stacked = jnp.stack([keys, values])
        piece = swap_partner(ring_gather(stacked, "sy", ny, 1), cores, 2)
        width = piece.shape[1]
        ring_tok = jnp.arange(width, dtype=jnp.int32)
        key_tokens = ((chip + ring_tok // chip_tokens) % ny) * chip_tokens + ring_tok % chip_tokens

        seq_pos = (chip * cores + core) * tok_count + jnp.arange(tok_count, dtype=jnp.int32)
        query_docs = lookup_docs(seq_pos, block_docs[0])
        key_heads = piece.shape[2] // HD
        group = queries.shape[2] // HD // key_heads
        query_heads = queries[0].reshape(tok_count, key_heads, group, HD)
        inv_root = 1.0 / jnp.sqrt(jnp.float32(HD))
        key_docs = lookup_docs(key_tokens, block_docs[0])
        same_doc = query_docs[:, None] == key_docs[None, :]
        run_max = jnp.full((key_heads, group, tok_count), -1e30, jnp.float32)
        key_part = piece[0].reshape(width, key_heads, HD)
        value_part = piece[1].reshape(width, key_heads, HD)
        scores = (
            jnp.einsum("tgjd,sgd->gjts", query_heads, key_part, preferred_element_type=jnp.float32)
            * inv_root
        )
        scores = jnp.where(same_doc[None, None], scores, jnp.float32(-1e30))
        new_max = jnp.maximum(run_max, jnp.max(scores, axis=-1))
        weight = jnp.where(same_doc[None, None], jnp.exp(scores - new_max[..., None]), jnp.float32(0.0))
        new_sum = jnp.sum(weight, axis=-1)
        update = jnp.einsum(
            "gjts,sgd->gjtd",
            weight.astype(jnp.bfloat16),
            value_part,
            preferred_element_type=jnp.float32,
        )
        result = update / new_sum[..., None]
        result = jnp.transpose(result, (2, 0, 1, 3)).reshape(tok_count, key_heads * group * HD)
        return result.astype(jnp.bfloat16)[None]

    return per_device


def solution(mesh):
    seq, fsdp, tp = (mesh.shape[name] for name in ("seq", "fsdp", "tp"))
    cores = 2
    x_size = 4
    fine = Mesh(
        mesh.devices.reshape(seq // cores, cores, fsdp // x_size, x_size, tp),
        ("sy", "sc", "fz", "fx", "tp"),
    )
    in_specs = (
        P(FSDP, SEQ, None),
        P(FSDP, SEQ, "tp"),
        P(None, FSDP, "tp"),
        P(None, "tp"),
        P(FSDP, None),
        P(FSDP, None),
    )
    out_specs = P(FSDP, SEQ, "tp")
    return jax.shard_map(
        make_per_device(cores), mesh=fine, in_specs=in_specs, out_specs=out_specs, check_vma=False
    )
```

```python
import jax
import jax.numpy as jnp
from jax import lax
from jax.sharding import Mesh
from jax.sharding import PartitionSpec as P

HD = 128
BLK = 128

SEQ = ("sy", "sc")
FSDP = ("fz", "fx")


def rotate_keys(key_heads, positions):
    half = key_heads.shape[-1] // 2
    freqs = jnp.exp(
        -jnp.arange(half, dtype=jnp.float32)
        * (2.0 / key_heads.shape[-1])
        * jnp.log(jnp.float32(1000000.0))
    )
    angle = positions.astype(jnp.float32)[:, None] * freqs[None, :]
    cosine = jnp.cos(angle)[:, None, :]
    sine = jnp.sin(angle)[:, None, :]
    first = key_heads[..., :half]
    second = key_heads[..., half:]
    return jnp.concatenate(
        [first * cosine - second * sine, second * cosine + first * sine], axis=-1
    )


def lookup_docs(token_index, block_table):
    block_index = token_index // BLK
    matches = block_index[:, None] == jnp.arange(block_table.shape[0], dtype=jnp.int32)[None, :]
    return jnp.sum(jnp.where(matches, block_table[None, :], 0), axis=1)


def doc_positions(token_index, doc_starts, block_docs):
    docs = lookup_docs(token_index, block_docs[0])
    doc_match = docs[:, None] == jnp.arange(doc_starts.shape[1], dtype=jnp.int32)[None, :]
    doc_first = jnp.sum(jnp.where(doc_match, doc_starts[0][None, :], 0), axis=1)
    return docs, token_index - doc_first


def shift(x, axis, size, step):
    return lax.ppermute(x, axis, [(i, (i + step) % size) for i in range(size)])


def ring_gather(piece, axis, size, dim, tie=None):
    half = piece.shape[dim] // 2
    from_prev = shift(piece, axis, size, 1)
    from_next = shift(piece, axis, size, -1)
    if tie is not None:
        from_prev, from_next, tie = lax.optimization_barrier((from_prev, from_next, tie))
    far_head = shift(lax.slice_in_dim(from_prev, 0, half, axis=dim), axis, size, 1)
    far_tail = shift(lax.slice_in_dim(from_next, half, 2 * half, axis=dim), axis, size, -1)
    out = jnp.concatenate([piece, from_next, far_head, far_tail, from_prev], axis=dim)
    return out if tie is None else (out, tie)


def swap_partner(x, cores, dim):
    core = lax.axis_index("sc")
    other = lax.ppermute(x, "sc", [(i, (i + 1) % cores) for i in range(cores)])
    return jnp.where(
        core == 0,
        jnp.concatenate([x, other], axis=dim),
        jnp.concatenate([other, x], axis=dim),
    )


def make_per_device(cores):
    def per_device(hidden, queries, w_kv, b_kv, doc_starts, block_docs):
        tok_count = hidden.shape[1]
        core = lax.axis_index("sc")
        chip = lax.axis_index("sy")
        nz, nx, ny = lax.axis_size("fz"), lax.axis_size("fx"), lax.axis_size("sy")
        fz, fx = lax.axis_index("fz"), lax.axis_index("fx")
        cols = w_kv.shape[2] // cores
        w_part = jnp.swapaxes(lax.dynamic_slice_in_dim(w_kv, core * cols, cols, axis=2), 1, 2)
        b_part = lax.dynamic_slice_in_dim(b_kv, core * cols, cols, axis=1)
        chip_rows = swap_partner(hidden[0], cores, 0)
        chip_tokens = chip_rows.shape[0]
        split = cols * 3 // 8
        w_sc = lax.all_gather(w_part[:, :split], FSDP, axis=2, tiled=True)
        blocks = nz * nx
        rows = w_part.shape[2]
        own_block = w_part[:, split:]
        fetch = [
            (y * nz + (z + y) % nz, y * nz + z) for y in range(1, ny) for z in range(nz)
        ]
        fetched = lax.ppermute(own_block, ("sy", "fz"), fetch)
        z_block = jnp.where(chip == 0, own_block, fetched)
        x_ring = ring_gather(z_block, "fx", nx, 2)
        ring_pos = jnp.arange(blocks, dtype=jnp.int32)
        ring_z = (fz + chip + ring_pos // nx) % nz
        ring_block = ring_z * nx + (fx + ring_pos % nx) % nx
        pick = (jnp.arange(blocks, dtype=jnp.int32)[:, None] == ring_block[None, :]).astype(chip_rows.dtype)
        ring_rows = jnp.einsum(
            "tbd,bp->tpd",
            chip_rows.reshape(chip_tokens, blocks, rows),
            pick,
            preferred_element_type=jnp.float32,
        ).astype(chip_rows.dtype).reshape(chip_tokens, blocks * rows)
        w_ring, ring_rows = ring_gather(x_ring, "sy", ny, 2, tie=ring_rows)
        kv_sc = jnp.einsum("td,ced->cte", chip_rows, w_sc, preferred_element_type=jnp.float32)
        kv_ring = jnp.einsum("td,ced->cte", ring_rows, w_ring, preferred_element_type=jnp.float32)
        key_value = jnp.concatenate([kv_sc, kv_ring], axis=2)
        key_value = key_value + b_part.astype(jnp.float32)[:, None, :]
        chip_pos = chip * chip_tokens + jnp.arange(chip_tokens, dtype=jnp.int32)
        _, positions = doc_positions(chip_pos, doc_starts, block_docs)
        part_heads = cols // HD
        rotated = rotate_keys(key_value[0].reshape(chip_tokens, part_heads, HD), positions)
        keys = rotated.astype(jnp.bfloat16).reshape(chip_tokens, cols)
        values = key_value[1].astype(jnp.bfloat16)
        stacked = jnp.stack([keys, values])
        piece = swap_partner(ring_gather(stacked, "sy", ny, 1), cores, 2)
        width = piece.shape[1]
        ring_tok = jnp.arange(width, dtype=jnp.int32)
        key_tokens = ((chip + ring_tok // chip_tokens) % ny) * chip_tokens + ring_tok % chip_tokens

        seq_pos = (chip * cores + core) * tok_count + jnp.arange(tok_count, dtype=jnp.int32)
        query_docs = lookup_docs(seq_pos, block_docs[0])
        key_heads = piece.shape[2] // HD
        group = queries.shape[2] // HD // key_heads
        query_heads = queries[0].reshape(tok_count, key_heads, group, HD)
        inv_root = 1.0 / jnp.sqrt(jnp.float32(HD))
        key_docs = lookup_docs(key_tokens, block_docs[0])
        same_doc = query_docs[:, None] == key_docs[None, :]
        run_max = jnp.full((key_heads, group, tok_count), -1e30, jnp.float32)
        key_part = piece[0].reshape(width, key_heads, HD)
        value_part = piece[1].reshape(width, key_heads, HD)
        scores = (
            jnp.einsum("tgjd,sgd->gjts", query_heads, key_part, preferred_element_type=jnp.float32)
            * inv_root
        )
        scores = jnp.where(same_doc[None, None], scores, jnp.float32(-1e30))
        new_max = jnp.maximum(run_max, jnp.max(scores, axis=-1))
        weight = jnp.where(same_doc[None, None], jnp.exp(scores - new_max[..., None]), jnp.float32(0.0))
        new_sum = jnp.sum(weight, axis=-1)
        update = jnp.einsum(
            "gjts,sgd->gjtd",
            weight.astype(jnp.bfloat16),
            value_part,
            preferred_element_type=jnp.float32,
        )
        result = update / new_sum[..., None]
        result = jnp.transpose(result, (2, 0, 1, 3)).reshape(tok_count, key_heads * group * HD)
        return result.astype(jnp.bfloat16)[None]

    return per_device


def solution(mesh):
    seq, fsdp, tp = (mesh.shape[name] for name in ("seq", "fsdp", "tp"))
    cores = 2
    x_size = 4
    fine = Mesh(
        mesh.devices.reshape(seq // cores, cores, fsdp // x_size, x_size, tp),
        ("sy", "sc", "fz", "fx", "tp"),
    )
    in_specs = (
        P(FSDP, SEQ, None),
        P(FSDP, SEQ, "tp"),
        P(None, FSDP, "tp"),
        P(None, "tp"),
        P(FSDP, None),
        P(FSDP, None),
    )
    out_specs = P(FSDP, SEQ, "tp")
    return jax.shard_map(
        make_per_device(cores), mesh=fine, in_specs=in_specs, out_specs=out_specs, check_vma=False
    )
```

```python
import jax
import jax.numpy as jnp
from jax import lax
from jax.sharding import Mesh
from jax.sharding import PartitionSpec as P

HD = 128
BLK = 128

SEQ = ("sy", "sc")
FSDP = ("fz", "fx")


def rotate_keys(key_heads, positions):
    half = key_heads.shape[-1] // 2
    freqs = jnp.exp(
        -jnp.arange(half, dtype=jnp.float32)
        * (2.0 / key_heads.shape[-1])
        * jnp.log(jnp.float32(1000000.0))
    )
    angle = positions.astype(jnp.float32)[:, None] * freqs[None, :]
    cosine = jnp.cos(angle)[:, None, :]
    sine = jnp.sin(angle)[:, None, :]
    first = key_heads[..., :half]
    second = key_heads[..., half:]
    return jnp.concatenate(
        [first * cosine - second * sine, second * cosine + first * sine], axis=-1
    )


def lookup_docs(token_index, block_table):
    block_index = token_index // BLK
    matches = block_index[:, None] == jnp.arange(block_table.shape[0], dtype=jnp.int32)[None, :]
    return jnp.sum(jnp.where(matches, block_table[None, :], 0), axis=1)


def doc_positions(token_index, doc_starts, block_docs):
    docs = lookup_docs(token_index, block_docs[0])
    doc_match = docs[:, None] == jnp.arange(doc_starts.shape[1], dtype=jnp.int32)[None, :]
    doc_first = jnp.sum(jnp.where(doc_match, doc_starts[0][None, :], 0), axis=1)
    return docs, token_index - doc_first


def shift(x, axis, size, step):
    return lax.ppermute(x, axis, [(i, (i + step) % size) for i in range(size)])


def ring_gather(piece, axis, size, dim, tie=None):
    half = piece.shape[dim] // 2
    from_prev = shift(piece, axis, size, 1)
    from_next = shift(piece, axis, size, -1)
    if tie is not None:
        from_prev, from_next, tie = lax.optimization_barrier((from_prev, from_next, tie))
    far_head = shift(lax.slice_in_dim(from_prev, 0, half, axis=dim), axis, size, 1)
    far_tail = shift(lax.slice_in_dim(from_next, half, 2 * half, axis=dim), axis, size, -1)
    out = jnp.concatenate([piece, from_next, far_head, far_tail, from_prev], axis=dim)
    return out if tie is None else (out, tie)


def swap_partner(x, cores, dim):
    core = lax.axis_index("sc")
    other = lax.ppermute(x, "sc", [(i, (i + 1) % cores) for i in range(cores)])
    return jnp.where(
        core == 0,
        jnp.concatenate([x, other], axis=dim),
        jnp.concatenate([other, x], axis=dim),
    )


def make_per_device(cores):
    def per_device(hidden, queries, w_kv, b_kv, doc_starts, block_docs):
        tok_count = hidden.shape[1]
        core = lax.axis_index("sc")
        chip = lax.axis_index("sy")
        nz, nx, ny = lax.axis_size("fz"), lax.axis_size("fx"), lax.axis_size("sy")
        fz, fx = lax.axis_index("fz"), lax.axis_index("fx")
        cols = w_kv.shape[2] // cores
        w_part = jnp.swapaxes(lax.dynamic_slice_in_dim(w_kv, core * cols, cols, axis=2), 1, 2)
        b_part = lax.dynamic_slice_in_dim(b_kv, core * cols, cols, axis=1)
        chip_rows = swap_partner(hidden[0], cores, 0)
        chip_tokens = chip_rows.shape[0]
        split = cols * 3 // 8
        w_sc = lax.all_gather(w_part[:, :split], FSDP, axis=2, tiled=True)
        blocks = nz * nx
        rows = w_part.shape[2]
        own_block = w_part[:, split:]
        fetch = [
            (y * nz + (z + y) % nz, y * nz + z) for y in range(1, ny) for z in range(nz)
        ]
        fetched = lax.ppermute(own_block, ("sy", "fz"), fetch)
        z_block = jnp.where(chip == 0, own_block, fetched)
        ring_half = (cols - split) // 2
        x_first = ring_gather(z_block[:, :ring_half], "fx", nx, 2)
        y_first = ring_gather(z_block[:, ring_half:], "sy", ny, 2)
        ring_pos = jnp.arange(blocks, dtype=jnp.int32)
        xf_block = ((fz + chip + ring_pos // nx) % nz) * nx + (fx + ring_pos % nx) % nx
        yf_block = ((fz + chip + ring_pos % ny) % nz) * nx + (fx + ring_pos // ny) % nx
        ring_block = jnp.concatenate([xf_block, yf_block])
        pick = (jnp.arange(blocks, dtype=jnp.int32)[:, None] == ring_block[None, :]).astype(chip_rows.dtype)
        ring_rows = jnp.einsum(
            "tbd,bp->tpd",
            chip_rows.reshape(chip_tokens, blocks, rows),
            pick,
            preferred_element_type=jnp.float32,
        ).astype(chip_rows.dtype).reshape(chip_tokens, 2, blocks * rows)
        w_xf, ring_rows = ring_gather(x_first, "sy", ny, 2, tie=ring_rows)
        w_yf = ring_gather(y_first, "fx", nx, 2)
        kv_xf = jnp.einsum("td,ced->cte", ring_rows[:, 0], w_xf, preferred_element_type=jnp.float32)
        kv_yf = jnp.einsum("td,ced->cte", ring_rows[:, 1], w_yf, preferred_element_type=jnp.float32)
        kv_ring = jnp.concatenate([kv_xf, kv_yf], axis=2)
        kv_sc = jnp.einsum("td,ced->cte", chip_rows, w_sc, preferred_element_type=jnp.float32)
        key_value = jnp.concatenate([kv_sc, kv_ring], axis=2)
        key_value = key_value + b_part.astype(jnp.float32)[:, None, :]
        chip_pos = chip * chip_tokens + jnp.arange(chip_tokens, dtype=jnp.int32)
        _, positions = doc_positions(chip_pos, doc_starts, block_docs)
        part_heads = cols // HD
        rotated = rotate_keys(key_value[0].reshape(chip_tokens, part_heads, HD), positions)
        keys = rotated.astype(jnp.bfloat16).reshape(chip_tokens, cols)
        values = key_value[1].astype(jnp.bfloat16)
        stacked = jnp.stack([keys, values])
        piece = swap_partner(ring_gather(stacked, "sy", ny, 1), cores, 2)
        width = piece.shape[1]
        ring_tok = jnp.arange(width, dtype=jnp.int32)
        key_tokens = ((chip + ring_tok // chip_tokens) % ny) * chip_tokens + ring_tok % chip_tokens

        seq_pos = (chip * cores + core) * tok_count + jnp.arange(tok_count, dtype=jnp.int32)
        query_docs = lookup_docs(seq_pos, block_docs[0])
        key_heads = piece.shape[2] // HD
        group = queries.shape[2] // HD // key_heads
        query_heads = queries[0].reshape(tok_count, key_heads, group, HD)
        inv_root = 1.0 / jnp.sqrt(jnp.float32(HD))
        key_docs = lookup_docs(key_tokens, block_docs[0])
        same_doc = query_docs[:, None] == key_docs[None, :]
        run_max = jnp.full((key_heads, group, tok_count), -1e30, jnp.float32)
        key_part = piece[0].reshape(width, key_heads, HD)
        value_part = piece[1].reshape(width, key_heads, HD)
        scores = (
            jnp.einsum("tgjd,sgd->gjts", query_heads, key_part, preferred_element_type=jnp.float32)
            * inv_root
        )
        scores = jnp.where(same_doc[None, None], scores, jnp.float32(-1e30))
        new_max = jnp.maximum(run_max, jnp.max(scores, axis=-1))
        weight = jnp.where(same_doc[None, None], jnp.exp(scores - new_max[..., None]), jnp.float32(0.0))
        new_sum = jnp.sum(weight, axis=-1)
        update = jnp.einsum(
            "gjts,sgd->gjtd",
            weight.astype(jnp.bfloat16),
            value_part,
            preferred_element_type=jnp.float32,
        )
        result = update / new_sum[..., None]
        result = jnp.transpose(result, (2, 0, 1, 3)).reshape(tok_count, key_heads * group * HD)
        return result.astype(jnp.bfloat16)[None]

    return per_device


def solution(mesh):
    seq, fsdp, tp = (mesh.shape[name] for name in ("seq", "fsdp", "tp"))
    cores = 2
    x_size = 4
    fine = Mesh(
        mesh.devices.reshape(seq // cores, cores, fsdp // x_size, x_size, tp),
        ("sy", "sc", "fz", "fx", "tp"),
    )
    in_specs = (
        P(FSDP, SEQ, None),
        P(FSDP, SEQ, "tp"),
        P(None, FSDP, "tp"),
        P(None, "tp"),
        P(FSDP, None),
        P(FSDP, None),
    )
    out_specs = P(FSDP, SEQ, "tp")
    return jax.shard_map(
        make_per_device(cores), mesh=fine, in_specs=in_specs, out_specs=out_specs, check_vma=False
    )
```

```python
import jax
import jax.numpy as jnp
from jax import lax
from jax.sharding import Mesh
from jax.sharding import PartitionSpec as P

HD = 128
BLK = 128

SEQ = ("sy", "sc")
FSDP = ("fz", "fx")


def rotate_keys(key_heads, positions):
    half = key_heads.shape[-1] // 2
    freqs = jnp.exp(
        -jnp.arange(half, dtype=jnp.float32)
        * (2.0 / key_heads.shape[-1])
        * jnp.log(jnp.float32(1000000.0))
    )
    angle = positions.astype(jnp.float32)[:, None] * freqs[None, :]
    cosine = jnp.cos(angle)[:, None, :]
    sine = jnp.sin(angle)[:, None, :]
    first = key_heads[..., :half]
    second = key_heads[..., half:]
    return jnp.concatenate(
        [first * cosine - second * sine, second * cosine + first * sine], axis=-1
    )


def lookup_docs(token_index, block_table):
    block_index = token_index // BLK
    matches = block_index[:, None] == jnp.arange(block_table.shape[0], dtype=jnp.int32)[None, :]
    return jnp.sum(jnp.where(matches, block_table[None, :], 0), axis=1)


def doc_positions(token_index, doc_starts, block_docs):
    docs = lookup_docs(token_index, block_docs[0])
    doc_match = docs[:, None] == jnp.arange(doc_starts.shape[1], dtype=jnp.int32)[None, :]
    doc_first = jnp.sum(jnp.where(doc_match, doc_starts[0][None, :], 0), axis=1)
    return docs, token_index - doc_first


def shift(x, axis, size, step):
    return lax.ppermute(x, axis, [(i, (i + step) % size) for i in range(size)])


def ring_gather(piece, axis, size, dim, tie=None):
    half = piece.shape[dim] // 2
    from_prev = shift(piece, axis, size, 1)
    from_next = shift(piece, axis, size, -1)
    if tie is not None:
        from_prev, from_next, tie = lax.optimization_barrier((from_prev, from_next, tie))
    far_head = shift(lax.slice_in_dim(from_prev, 0, half, axis=dim), axis, size, 1)
    far_tail = shift(lax.slice_in_dim(from_next, half, 2 * half, axis=dim), axis, size, -1)
    out = jnp.concatenate([piece, from_next, far_head, far_tail, from_prev], axis=dim)
    return out if tie is None else (out, tie)


def swap_partner(x, cores, dim):
    core = lax.axis_index("sc")
    other = lax.ppermute(x, "sc", [(i, (i + 1) % cores) for i in range(cores)])
    return jnp.where(
        core == 0,
        jnp.concatenate([x, other], axis=dim),
        jnp.concatenate([other, x], axis=dim),
    )


def make_per_device(cores):
    def per_device(hidden, queries, w_kv, b_kv, doc_starts, block_docs):
        tok_count = hidden.shape[1]
        core = lax.axis_index("sc")
        chip = lax.axis_index("sy")
        nz, nx, ny = lax.axis_size("fz"), lax.axis_size("fx"), lax.axis_size("sy")
        fz, fx = lax.axis_index("fz"), lax.axis_index("fx")
        cols = w_kv.shape[2] // cores
        w_part = jnp.swapaxes(lax.dynamic_slice_in_dim(w_kv, core * cols, cols, axis=2), 1, 2)
        b_part = lax.dynamic_slice_in_dim(b_kv, core * cols, cols, axis=1)
        chip_rows = swap_partner(hidden[0], cores, 0)
        chip_tokens = chip_rows.shape[0]
        split = cols * 3 // 8
        w_sc = lax.all_gather(w_part[:, :split], FSDP, axis=2, tiled=True)
        blocks = nz * nx
        rows = w_part.shape[2]
        own_block = w_part[:, split:]
        near = [
            (y * nz + (z + y) % nz, y * nz + z) for y in (1, ny - 1) for z in range(nz)
        ]
        fetched = lax.ppermute(own_block, ("sy", "fz"), near)
        far_row = 2

        def relay(x, step):
            pairs = [(far_row * nz + (z + step) % nz, far_row * nz + z) for z in range(nz)]
            return lax.ppermute(x, ("sy", "fz"), pairs)

        half_rows = rows // 2
        far_head = relay(relay(own_block[..., :half_rows], 1), 1)
        far_tail = relay(relay(own_block[..., half_rows:], -1), -1)
        far_block = jnp.concatenate([far_head, far_tail], axis=2)
        z_block = jnp.where(chip == 0, own_block, jnp.where(chip == far_row, far_block, fetched))
        x_ring = ring_gather(z_block, "fx", nx, 2)
        ring_pos = jnp.arange(blocks, dtype=jnp.int32)
        ring_z = (fz + chip + ring_pos // nx) % nz
        ring_block = ring_z * nx + (fx + ring_pos % nx) % nx
        pick = (jnp.arange(blocks, dtype=jnp.int32)[:, None] == ring_block[None, :]).astype(chip_rows.dtype)
        ring_rows = jnp.einsum(
            "tbd,bp->tpd",
            chip_rows.reshape(chip_tokens, blocks, rows),
            pick,
            preferred_element_type=jnp.float32,
        ).astype(chip_rows.dtype).reshape(chip_tokens, blocks * rows)
        w_ring, ring_rows = ring_gather(x_ring, "sy", ny, 2, tie=ring_rows)
        kv_sc = jnp.einsum("td,ced->cte", chip_rows, w_sc, preferred_element_type=jnp.float32)
        kv_ring = jnp.einsum("td,ced->cte", ring_rows, w_ring, preferred_element_type=jnp.float32)
        key_value = jnp.concatenate([kv_sc, kv_ring], axis=2)
        key_value = key_value + b_part.astype(jnp.float32)[:, None, :]
        chip_pos = chip * chip_tokens + jnp.arange(chip_tokens, dtype=jnp.int32)
        _, positions = doc_positions(chip_pos, doc_starts, block_docs)
        part_heads = cols // HD
        rotated = rotate_keys(key_value[0].reshape(chip_tokens, part_heads, HD), positions)
        keys = rotated.astype(jnp.bfloat16).reshape(chip_tokens, cols)
        values = key_value[1].astype(jnp.bfloat16)
        stacked = jnp.stack([keys, values])
        piece = swap_partner(ring_gather(stacked, "sy", ny, 1), cores, 2)
        width = piece.shape[1]
        ring_tok = jnp.arange(width, dtype=jnp.int32)
        key_tokens = ((chip + ring_tok // chip_tokens) % ny) * chip_tokens + ring_tok % chip_tokens

        seq_pos = (chip * cores + core) * tok_count + jnp.arange(tok_count, dtype=jnp.int32)
        query_docs = lookup_docs(seq_pos, block_docs[0])
        key_heads = piece.shape[2] // HD
        group = queries.shape[2] // HD // key_heads
        query_heads = queries[0].reshape(tok_count, key_heads, group, HD)
        inv_root = 1.0 / jnp.sqrt(jnp.float32(HD))
        key_docs = lookup_docs(key_tokens, block_docs[0])
        same_doc = query_docs[:, None] == key_docs[None, :]
        run_max = jnp.full((key_heads, group, tok_count), -1e30, jnp.float32)
        key_part = piece[0].reshape(width, key_heads, HD)
        value_part = piece[1].reshape(width, key_heads, HD)
        scores = (
            jnp.einsum("tgjd,sgd->gjts", query_heads, key_part, preferred_element_type=jnp.float32)
            * inv_root
        )
        scores = jnp.where(same_doc[None, None], scores, jnp.float32(-1e30))
        new_max = jnp.maximum(run_max, jnp.max(scores, axis=-1))
        weight = jnp.where(same_doc[None, None], jnp.exp(scores - new_max[..., None]), jnp.float32(0.0))
        new_sum = jnp.sum(weight, axis=-1)
        update = jnp.einsum(
            "gjts,sgd->gjtd",
            weight.astype(jnp.bfloat16),
            value_part,
            preferred_element_type=jnp.float32,
        )
        result = update / new_sum[..., None]
        result = jnp.transpose(result, (2, 0, 1, 3)).reshape(tok_count, key_heads * group * HD)
        return result.astype(jnp.bfloat16)[None]

    return per_device


def solution(mesh):
    seq, fsdp, tp = (mesh.shape[name] for name in ("seq", "fsdp", "tp"))
    cores = 2
    x_size = 4
    fine = Mesh(
        mesh.devices.reshape(seq // cores, cores, fsdp // x_size, x_size, tp),
        ("sy", "sc", "fz", "fx", "tp"),
    )
    in_specs = (
        P(FSDP, SEQ, None),
        P(FSDP, SEQ, "tp"),
        P(None, FSDP, "tp"),
        P(None, "tp"),
        P(FSDP, None),
        P(FSDP, None),
    )
    out_specs = P(FSDP, SEQ, "tp")
    return jax.shard_map(
        make_per_device(cores), mesh=fine, in_specs=in_specs, out_specs=out_specs, check_vma=False
    )
```

```python
import jax
import jax.numpy as jnp
from jax import lax
from jax.sharding import Mesh
from jax.sharding import PartitionSpec as P

HD = 128
BLK = 128

SEQ = ("sy", "sc")
FSDP = ("fz", "fx")


def rotate_keys(key_heads, positions):
    half = key_heads.shape[-1] // 2
    freqs = jnp.exp(
        -jnp.arange(half, dtype=jnp.float32)
        * (2.0 / key_heads.shape[-1])
        * jnp.log(jnp.float32(1000000.0))
    )
    angle = positions.astype(jnp.float32)[:, None] * freqs[None, :]
    cosine = jnp.cos(angle)[:, None, :]
    sine = jnp.sin(angle)[:, None, :]
    first = key_heads[..., :half]
    second = key_heads[..., half:]
    return jnp.concatenate(
        [first * cosine - second * sine, second * cosine + first * sine], axis=-1
    )


def lookup_docs(token_index, block_table):
    block_index = token_index // BLK
    matches = block_index[:, None] == jnp.arange(block_table.shape[0], dtype=jnp.int32)[None, :]
    return jnp.sum(jnp.where(matches, block_table[None, :], 0), axis=1)


def doc_positions(token_index, doc_starts, block_docs):
    docs = lookup_docs(token_index, block_docs[0])
    doc_match = docs[:, None] == jnp.arange(doc_starts.shape[1], dtype=jnp.int32)[None, :]
    doc_first = jnp.sum(jnp.where(doc_match, doc_starts[0][None, :], 0), axis=1)
    return docs, token_index - doc_first


def shift(x, axis, size, step):
    return lax.ppermute(x, axis, [(i, (i + step) % size) for i in range(size)])


def ring_gather(piece, axis, size, dim, tie=None):
    half = piece.shape[dim] // 2
    from_prev = shift(piece, axis, size, 1)
    from_next = shift(piece, axis, size, -1)
    if tie is not None:
        from_prev, from_next, tie = lax.optimization_barrier((from_prev, from_next, tie))
    far_head = shift(lax.slice_in_dim(from_prev, 0, half, axis=dim), axis, size, 1)
    far_tail = shift(lax.slice_in_dim(from_next, half, 2 * half, axis=dim), axis, size, -1)
    out = jnp.concatenate([piece, from_next, far_head, far_tail, from_prev], axis=dim)
    return out if tie is None else (out, tie)


def swap_partner(x, cores, dim):
    core = lax.axis_index("sc")
    other = lax.ppermute(x, "sc", [(i, (i + 1) % cores) for i in range(cores)])
    return jnp.where(
        core == 0,
        jnp.concatenate([x, other], axis=dim),
        jnp.concatenate([other, x], axis=dim),
    )


def make_per_device(cores):
    def per_device(hidden, queries, w_kv, b_kv, doc_starts, block_docs):
        tok_count = hidden.shape[1]
        core = lax.axis_index("sc")
        chip = lax.axis_index("sy")
        nz, nx, ny = lax.axis_size("fz"), lax.axis_size("fx"), lax.axis_size("sy")
        fz, fx = lax.axis_index("fz"), lax.axis_index("fx")
        cols = w_kv.shape[2] // cores
        w_part = jnp.swapaxes(lax.dynamic_slice_in_dim(w_kv, core * cols, cols, axis=2), 1, 2)
        b_part = lax.dynamic_slice_in_dim(b_kv, core * cols, cols, axis=1)
        chip_rows = swap_partner(hidden[0], cores, 0)
        chip_tokens = chip_rows.shape[0]
        split = cols * 3 // 8
        w_sc = lax.all_gather(w_part[:, :split], FSDP, axis=2, tiled=True)
        blocks = nz * nx
        rows = w_part.shape[2]
        own_block = w_part[:, split:]
        fetch = [
            (y * nz + (z + y) % nz, y * nz + z) for y in range(1, ny) for z in range(nz)
        ]
        fetched = lax.ppermute(own_block, ("sy", "fz"), fetch)
        z_block = jnp.where(chip == 0, own_block, fetched)
        x_ring = ring_gather(z_block, "fx", nx, 2)
        ring_pos = jnp.arange(blocks, dtype=jnp.int32)
        ring_z = (fz + chip + ring_pos // nx) % nz
        ring_block = ring_z * nx + (fx + ring_pos % nx) % nx
        pick = (jnp.arange(blocks, dtype=jnp.int32)[:, None] == ring_block[None, :]).astype(chip_rows.dtype)
        ring_rows = jnp.einsum(
            "tbd,bp->tpd",
            chip_rows.reshape(chip_tokens, blocks, rows),
            pick,
            preferred_element_type=jnp.float32,
        ).astype(chip_rows.dtype).reshape(chip_tokens, blocks * rows)
        w_ring, ring_rows = ring_gather(x_ring, "sy", ny, 2, tie=ring_rows)
        kv_sc = jnp.einsum("td,ced->cte", chip_rows, w_sc, preferred_element_type=jnp.float32)
        kv_ring = jnp.einsum("td,ced->cte", ring_rows, w_ring, preferred_element_type=jnp.float32)
        key_value = jnp.concatenate([kv_sc, kv_ring], axis=2)
        key_value = key_value + b_part.astype(jnp.float32)[:, None, :]
        chip_pos = chip * chip_tokens + jnp.arange(chip_tokens, dtype=jnp.int32)
        _, positions = doc_positions(chip_pos, doc_starts, block_docs)
        part_heads = cols // HD
        rotated = rotate_keys(key_value[0].reshape(chip_tokens, part_heads, HD), positions)
        keys = rotated.astype(jnp.bfloat16).reshape(chip_tokens, cols)
        values = key_value[1].astype(jnp.bfloat16)
        stacked = jnp.stack([keys, values])
        piece = swap_partner(ring_gather(stacked, "sy", ny, 1), cores, 2)
        seq_pos = (chip * cores + core) * tok_count + jnp.arange(tok_count, dtype=jnp.int32)
        query_docs = lookup_docs(seq_pos, block_docs[0])
        skip_chip = jnp.where(query_docs[0] == 0, ny - 1, 0)
        first = (skip_chip - chip + 1) % ny
        keep = ny - 1
        doubled = jnp.concatenate([piece, piece], axis=1)
        piece = lax.dynamic_slice_in_dim(doubled, first * chip_tokens, keep * chip_tokens, axis=1)
        width = piece.shape[1]
        ring_tok = jnp.arange(width, dtype=jnp.int32)
        key_chip = (chip + first + ring_tok // chip_tokens) % ny
        key_tokens = key_chip * chip_tokens + ring_tok % chip_tokens

        key_heads = piece.shape[2] // HD
        group = queries.shape[2] // HD // key_heads
        query_heads = queries[0].reshape(tok_count, key_heads, group, HD)
        inv_root = 1.0 / jnp.sqrt(jnp.float32(HD))
        key_docs = lookup_docs(key_tokens, block_docs[0])
        same_doc = query_docs[:, None] == key_docs[None, :]
        run_max = jnp.full((key_heads, group, tok_count), -1e30, jnp.float32)
        key_part = piece[0].reshape(width, key_heads, HD)
        value_part = piece[1].reshape(width, key_heads, HD)
        scores = (
            jnp.einsum("tgjd,sgd->gjts", query_heads, key_part, preferred_element_type=jnp.float32)
            * inv_root
        )
        scores = jnp.where(same_doc[None, None], scores, jnp.float32(-1e30))
        new_max = jnp.maximum(run_max, jnp.max(scores, axis=-1))
        weight = jnp.where(same_doc[None, None], jnp.exp(scores - new_max[..., None]), jnp.float32(0.0))
        new_sum = jnp.sum(weight, axis=-1)
        update = jnp.einsum(
            "gjts,sgd->gjtd",
            weight.astype(jnp.bfloat16),
            value_part,
            preferred_element_type=jnp.float32,
        )
        result = update / new_sum[..., None]
        result = jnp.transpose(result, (2, 0, 1, 3)).reshape(tok_count, key_heads * group * HD)
        return result.astype(jnp.bfloat16)[None]

    return per_device


def solution(mesh):
    seq, fsdp, tp = (mesh.shape[name] for name in ("seq", "fsdp", "tp"))
    cores = 2
    x_size = 4
    fine = Mesh(
        mesh.devices.reshape(seq // cores, cores, fsdp // x_size, x_size, tp),
        ("sy", "sc", "fz", "fx", "tp"),
    )
    in_specs = (
        P(FSDP, SEQ, None),
        P(FSDP, SEQ, "tp"),
        P(None, FSDP, "tp"),
        P(None, "tp"),
        P(FSDP, None),
        P(FSDP, None),
    )
    out_specs = P(FSDP, SEQ, "tp")
    return jax.shard_map(
        make_per_device(cores), mesh=fine, in_specs=in_specs, out_specs=out_specs, check_vma=False
    )
```

```python
import jax
import jax.numpy as jnp
from jax import lax
from jax.sharding import Mesh
from jax.sharding import PartitionSpec as P

HD = 128
BLK = 128

SEQ = ("sy", "sc")
FSDP = ("fz", "fx")


def rotate_keys(key_heads, positions):
    half = key_heads.shape[-1] // 2
    freqs = jnp.exp(
        -jnp.arange(half, dtype=jnp.float32)
        * (2.0 / key_heads.shape[-1])
        * jnp.log(jnp.float32(1000000.0))
    )
    angle = positions.astype(jnp.float32)[:, None] * freqs[None, :]
    cosine = jnp.cos(angle)[:, None, :]
    sine = jnp.sin(angle)[:, None, :]
    first = key_heads[..., :half]
    second = key_heads[..., half:]
    return jnp.concatenate(
        [first * cosine - second * sine, second * cosine + first * sine], axis=-1
    )


def lookup_docs(token_index, block_table):
    block_index = token_index // BLK
    matches = block_index[:, None] == jnp.arange(block_table.shape[0], dtype=jnp.int32)[None, :]
    return jnp.sum(jnp.where(matches, block_table[None, :], 0), axis=1)


def doc_positions(token_index, doc_starts, block_docs):
    docs = lookup_docs(token_index, block_docs[0])
    doc_match = docs[:, None] == jnp.arange(doc_starts.shape[1], dtype=jnp.int32)[None, :]
    doc_first = jnp.sum(jnp.where(doc_match, doc_starts[0][None, :], 0), axis=1)
    return docs, token_index - doc_first


def shift(x, axis, size, step):
    return lax.ppermute(x, axis, [(i, (i + step) % size) for i in range(size)])


def ring_gather(piece, axis, size, dim, tie=None):
    half = piece.shape[dim] // 2
    from_prev = shift(piece, axis, size, 1)
    from_next = shift(piece, axis, size, -1)
    if tie is not None:
        from_prev, from_next, tie = lax.optimization_barrier((from_prev, from_next, tie))
    far_head = shift(lax.slice_in_dim(from_prev, 0, half, axis=dim), axis, size, 1)
    far_tail = shift(lax.slice_in_dim(from_next, half, 2 * half, axis=dim), axis, size, -1)
    out = jnp.concatenate([piece, from_next, far_head, far_tail, from_prev], axis=dim)
    return out if tie is None else (out, tie)


def swap_partner(x, cores, dim):
    core = lax.axis_index("sc")
    other = lax.ppermute(x, "sc", [(i, (i + 1) % cores) for i in range(cores)])
    return jnp.where(
        core == 0,
        jnp.concatenate([x, other], axis=dim),
        jnp.concatenate([other, x], axis=dim),
    )


def make_per_device(cores):
    def per_device(hidden, queries, w_kv, b_kv, doc_starts, block_docs):
        tok_count = hidden.shape[1]
        core = lax.axis_index("sc")
        chip = lax.axis_index("sy")
        nz, nx, ny = lax.axis_size("fz"), lax.axis_size("fx"), lax.axis_size("sy")
        fz, fx = lax.axis_index("fz"), lax.axis_index("fx")
        cols = w_kv.shape[2] // cores
        w_part = jnp.swapaxes(lax.dynamic_slice_in_dim(w_kv, core * cols, cols, axis=2), 1, 2)
        b_part = lax.dynamic_slice_in_dim(b_kv, core * cols, cols, axis=1)
        chip_rows = swap_partner(hidden[0], cores, 0)
        chip_tokens = chip_rows.shape[0]
        split = cols * 3 // 8
        w_sc = lax.all_gather(w_part[:, :split], FSDP, axis=2, tiled=True)
        blocks = nz * nx
        rows = w_part.shape[2]
        own_block = w_part[:, split:]
        fetch = [
            (y * nz + (z + y) % nz, y * nz + z) for y in range(1, ny) for z in range(nz)
        ]
        fetched = lax.ppermute(own_block, ("sy", "fz"), fetch)
        z_block = jnp.where(chip == 0, own_block, fetched)
        x_ring = ring_gather(z_block, "fx", nx, 2)
        ring_pos = jnp.arange(blocks, dtype=jnp.int32)
        ring_z = (fz + chip + ring_pos // nx) % nz
        ring_block = ring_z * nx + (fx + ring_pos % nx) % nx
        pick = (jnp.arange(blocks, dtype=jnp.int32)[:, None] == ring_block[None, :]).astype(chip_rows.dtype)
        ring_rows = jnp.einsum(
            "tbd,bp->tpd",
            chip_rows.reshape(chip_tokens, blocks, rows),
            pick,
            preferred_element_type=jnp.float32,
        ).astype(chip_rows.dtype).reshape(chip_tokens, blocks * rows)
        w_ring, ring_rows = ring_gather(x_ring, "sy", ny, 2, tie=ring_rows)
        kv_sc = jnp.einsum("td,ced->cte", chip_rows, w_sc, preferred_element_type=jnp.float32)
        kv_ring = jnp.einsum("td,ced->cte", ring_rows, w_ring, preferred_element_type=jnp.float32)
        key_value = jnp.concatenate([kv_sc, kv_ring], axis=2)
        key_value = key_value + b_part.astype(jnp.float32)[:, None, :]
        chip_pos = chip * chip_tokens + jnp.arange(chip_tokens, dtype=jnp.int32)
        _, positions = doc_positions(chip_pos, doc_starts, block_docs)
        part_heads = cols // HD
        rotated = rotate_keys(key_value[0].reshape(chip_tokens, part_heads, HD), positions)
        keys = rotated.astype(jnp.bfloat16).reshape(chip_tokens, cols)
        values = key_value[1].astype(jnp.bfloat16)
        stacked = jnp.stack([keys, values])
        ring_kv = ring_gather(stacked, "sy", ny, 1)
        seq_pos = (chip * cores + core) * tok_count + jnp.arange(tok_count, dtype=jnp.int32)
        query_docs = lookup_docs(seq_pos, block_docs[0])
        skip_chip = jnp.where(query_docs[0] == 0, ny - 1, 0)
        first = (skip_chip - chip + 1) % ny
        keep = ny - 1
        doubled = jnp.concatenate([ring_kv, ring_kv], axis=1)
        window = lax.dynamic_slice_in_dim(doubled, first * chip_tokens, keep * chip_tokens, axis=1)
        piece = swap_partner(window, cores, 2)
        width = piece.shape[1]
        ring_tok = jnp.arange(width, dtype=jnp.int32)
        key_chip = (chip + first + ring_tok // chip_tokens) % ny
        key_tokens = key_chip * chip_tokens + ring_tok % chip_tokens

        key_heads = piece.shape[2] // HD
        group = queries.shape[2] // HD // key_heads
        query_heads = queries[0].reshape(tok_count, key_heads, group, HD)
        inv_root = 1.0 / jnp.sqrt(jnp.float32(HD))
        key_docs = lookup_docs(key_tokens, block_docs[0])
        same_doc = query_docs[:, None] == key_docs[None, :]
        run_max = jnp.full((key_heads, group, tok_count), -1e30, jnp.float32)
        key_part = piece[0].reshape(width, key_heads, HD)
        value_part = piece[1].reshape(width, key_heads, HD)
        scores = (
            jnp.einsum("tgjd,sgd->gjts", query_heads, key_part, preferred_element_type=jnp.float32)
            * inv_root
        )
        scores = jnp.where(same_doc[None, None], scores, jnp.float32(-1e30))
        new_max = jnp.maximum(run_max, jnp.max(scores, axis=-1))
        weight = jnp.where(same_doc[None, None], jnp.exp(scores - new_max[..., None]), jnp.float32(0.0))
        new_sum = jnp.sum(weight, axis=-1)
        update = jnp.einsum(
            "gjts,sgd->gjtd",
            weight.astype(jnp.bfloat16),
            value_part,
            preferred_element_type=jnp.float32,
        )
        result = update / new_sum[..., None]
        result = jnp.transpose(result, (2, 0, 1, 3)).reshape(tok_count, key_heads * group * HD)
        return result.astype(jnp.bfloat16)[None]

    return per_device


def solution(mesh):
    seq, fsdp, tp = (mesh.shape[name] for name in ("seq", "fsdp", "tp"))
    cores = 2
    x_size = 4
    fine = Mesh(
        mesh.devices.reshape(seq // cores, cores, fsdp // x_size, x_size, tp),
        ("sy", "sc", "fz", "fx", "tp"),
    )
    in_specs = (
        P(FSDP, SEQ, None),
        P(FSDP, SEQ, "tp"),
        P(None, FSDP, "tp"),
        P(None, "tp"),
        P(FSDP, None),
        P(FSDP, None),
    )
    out_specs = P(FSDP, SEQ, "tp")
    return jax.shard_map(
        make_per_device(cores), mesh=fine, in_specs=in_specs, out_specs=out_specs, check_vma=False
    )
```
